256 devices in a mesh: view: 32 (over y, z), brick: 8 (over x, core).
Axes of the slice: x: 4, y: 4, z: 8, core: 2. Of those that a mesh axis runs over, the one named last changes fastest.
Arguments:
- volume: float32 [16, 8, 32, 128], P('brick'), may hold values from -6 to 6
- offsets: float32 [32, 3], P('view'), may hold values from 0 to 1
- shifts: int32 [32, 2], P('view'), may hold values from 0 to 127
- order: int32 [32], P('view'), may hold values from 0 to 1
- cond: float32 [32, 8], P('view'), may hold values from -6 to 6
- w_in: float32 [16, 128], replicated, may hold values from -1.5 to 1.5
- w_mid: float32 [128, 128], replicated, may hold values from -0.5 to 0.5
- w_out: float32 [128, 4], replicated, may hold values from -0.5 to 0.5
- cot_image: float32 [32, 3, 32, 128], P('view', None, 'brick'), may hold values from -0.12 to 0.12
Outputs:
- image: float32 [32, 3, 32, 128], P('view', None, 'brick')
- grad_in: float32 [16, 128], replicated
- grad_mid: float32 [128, 128], replicated
- grad_out: float32 [128, 4], replicated
The draws below stay inside these ranges and needn't reach their ends.
Inputs may be any that keep to these rules, and one draw needn't show every extreme that they name: `order`: 0 marches towards higher slice numbers, 1 towards lower ones.
All inputs are finite; a program needn't handle non-finite values.
Results may differ from the reference program's by a relative error of at most 0.0003.
Values sent between devices are 32-bit elements; how exact they have to be, the bound alone decides.
No kernel may reach another device: no remote copies, remote signals or barrier semaphores. Data moves between devices by JAX's collectives and lax.ppermute only.
A program may use at most 64 MiB of HBM per device.

```python
import jax
import jax.numpy as jnp
from jax import lax

PX = 32
PY = 128
CH = 8
COND = 8
HID = 128
FIN = 16
VIEWS = 32
NZ = 16


def touch_ends(values, own_key, low, top_value):
    place = [jax.random.randint(jax.random.fold_in(own_key, axis), (), 0, length) for axis, length in enumerate(values.shape)]
    widest = values.shape.index(max(values.shape))
    beside = place[:widest] + [(place[widest] + 1) % values.shape[widest]] + place[widest + 1:]
    return values.at[tuple(place)].set(low).at[tuple(beside)].set(top_value)


def levels(own_key, shape, cuts, least, high):
    loudness, own = 1.0, jax.random.fold_in(own_key, 6)
    for position, blocks in cuts:
        draws = jnp.exp(jax.random.uniform(jax.random.fold_in(own, position), (blocks,), jnp.float32, least / len(cuts), high / len(cuts)))
        loudness = loudness * jnp.repeat(draws, shape[position] // blocks).reshape([-1 if axis == position else 1 for axis in range(len(shape))])
    return loudness


def normal_values(stream_key, shape, scale, bound, cuts=(), kind=jnp.bfloat16):
    gain = levels(stream_key, shape, cuts, -0.22, 0.18) if cuts else 1.0
    entries = jax.random.normal(stream_key, shape, jnp.float32) * scale * gain
    return jnp.minimum(jnp.maximum(entries, -bound), bound).astype(kind)


def setup_inputs(seed: int = 0) -> dict:
    splits = jax.random.split(jax.random.key(seed), 10)
    volume = normal_values(splits[0], (NZ, CH, PX, PY), 1.0, 6.0, ((0, 8),), jnp.float32)
    offsets = jnp.clip(1.0 * jax.random.uniform(splits[1], (VIEWS, 3), jnp.float32) ** levels(splits[1], (VIEWS, 3), ((0, 32),), -0.2, 0.2), 0.0, 1.0)
    shifts = touch_ends(jax.random.randint(splits[2], (VIEWS, 2), 0, PY), jax.random.fold_in(splits[2], 1), 0, PY - 1).astype(jnp.int32)
    order = touch_ends(jax.random.randint(splits[3], (VIEWS,), 0, 2), jax.random.fold_in(splits[3], 1), 0, 1).astype(jnp.int32)
    cond = normal_values(splits[4], (VIEWS, COND), 1.0, 6.0, ((0, 32),), jnp.float32)
    w_in = normal_values(splits[5], (FIN, HID), FIN ** -0.5, 1.5, (), jnp.float32)
    w_mid = normal_values(splits[6], (HID, HID), HID ** -0.5, 0.5, (), jnp.float32)
    w_out = normal_values(splits[7], (HID, 4), HID ** -0.5, 0.5, (), jnp.float32)
    cot_image = normal_values(splits[8], (VIEWS, 3, PX, PY), 0.02, 0.12, ((0, 32), (2, 8)), jnp.float32)
    return dict(volume=volume, offsets=offsets, shifts=shifts, order=order, cond=cond, w_in=w_in, w_mid=w_mid, w_out=w_out, cot_image=cot_image)


STEP_DEPTH = 0.15
precise = lax.Precision.HIGHEST

def resample(padded, shift_view, fraction):
    depthwise = (1.0 - fraction[2]) * padded[:-1] + fraction[2] * padded[1:]
    shifted = jnp.roll(depthwise, -shift_view[0], 2)
    shifted = (1.0 - fraction[0]) * shifted + fraction[0] * jnp.roll(shifted, -1, 2)
    columns = jnp.roll(shifted, -shift_view[1], 3)
    return (1.0 - fraction[1]) * columns + fraction[1] * jnp.roll(columns, -1, 3)

def transfer(weights, density, condition):
    w_in, w_mid, w_out = weights
    spread = jnp.broadcast_to(condition[:, None], (condition.shape[0], density.shape[1]))
    features = jnp.concatenate([density, spread], 0)
    hidden = jax.nn.silu(jnp.einsum('io,in->on', w_in, features, precision=precise))
    hidden = jax.nn.silu(jnp.einsum('io,in->on', w_mid, hidden, precision=precise))
    result = jnp.einsum('io,in->on', w_out, hidden, precision=precise)
    return jnp.concatenate([jax.nn.softplus(result[:1]), jax.nn.sigmoid(result[1:])], 0)

def composite(emitted):
    optical = emitted[:, 0] * STEP_DEPTH
    optical_depth = jnp.cumsum(optical, 0)
    transmit = jnp.exp(optical - optical_depth)
    opacity = -jnp.expm1(-optical)
    colour = lax.optimization_barrier(jnp.sum((transmit * opacity)[:, None] * emitted[:, 1:], 0))
    return (colour, jnp.exp(-optical_depth[-1]))

def render(weights, volume, shift_view, fraction, facing, condition):
    padded = jnp.concatenate([volume, jnp.zeros_like(volume[:1])], 0)
    samples = resample(padded, shift_view, fraction)
    slices, channels, rows_all, cols_all = samples.shape
    flat = samples.transpose(1, 0, 2, 3).reshape(channels, slices * rows_all * cols_all)
    emitted = transfer(weights, flat, condition)
    emitted = emitted.reshape(4, slices, rows_all * cols_all).transpose(1, 0, 2)
    marching = jnp.where(facing == 1, emitted[::-1], emitted)
    colour, _ = composite(marching)
    return colour.reshape(3, rows_all, cols_all)

def reference(volume, offsets, shifts, order, cond, w_in, w_mid, w_out, cot_image):
    weights = (w_in, w_mid, w_out)

    def one_view(summed, element):
        fraction, shift_view, facing, condition, cotangent = element
        picture, pullback = jax.vjp(lambda params: render(params, volume, shift_view, fraction, facing, condition), weights)
        gradients = pullback(cotangent)[0]
        return (jax.tree.map(jnp.add, summed, gradients), picture)
    initial = jax.tree.map(jnp.zeros_like, weights)
    summed, pictures = lax.scan(one_view, initial, (offsets, shifts, order, cond, cot_image))
    return (pictures, summed[0], summed[1], summed[2])
```

```python
import functools

import jax
import jax.numpy as jnp
from jax import lax
from jax.experimental import pallas as pl
from jax.experimental.pallas import tpu as pltpu
from jax.sharding import Mesh
from jax.sharding import PartitionSpec as P

VIEW = ("y_far", "y_near", "z")
BRICK = ("x", "core")
NEAR = ("y_near", "x", "core")
FAR = ("y_far", "z")

STEP_DEPTH = 0.15
NZ, CH, COND, HID = 16, 8, 8, 128
PX, PY = 32, 128
ROWS = 4
RAYS = ROWS * PY
PIECES, PIECE_ROWS = 16, 16
UNROLL = 2

bf16, f32 = jnp.bfloat16, jnp.float32
VMEM = pl.BlockSpec(memory_space=pltpu.VMEM)
SMEM = pl.BlockSpec(memory_space=pltpu.SMEM)


def split(value):
    high = value.astype(bf16)
    return high, (value - high.astype(f32)).astype(bf16)


def split3(value):
    high = value.astype(bf16).astype(f32)
    rest = value - high
    middle = rest.astype(bf16).astype(f32)
    return high, middle, rest - middle


def mul(a, b):
    return jnp.dot(a, b, preferred_element_type=f32)


def mul_t(a, b):
    return lax.dot_general(a, b, (((1,), (1,)), ((), ())), preferred_element_type=f32)


def two_halves(value):
    return value[: value.shape[0] // 2] + value[value.shape[0] // 2 :]


def two_sides(value):
    return value[:, : value.shape[1] // 2] + value[:, value.shape[1] // 2 :]


def get(ref, rows):
    return jnp.concatenate([ref[r, rows, :] for r in range(ROWS)], 1)


def put(ref, rows, value):
    for r in range(ROWS):
        ref[r, rows, :] = value[:, r * PY : (r + 1) * PY]


def resample_kernel(offsets, shifts, volume, out):
    f_row, f_col = offsets[0, 0], offsets[0, 1]
    row_shift = shifts[0, 0] & (PX - 1)
    col_shift = shifts[0, 1] & (PY - 1)
    roll_near = (PY - col_shift) & (PY - 1)
    roll_far = (PY - 1 - col_shift) & (PY - 1)

    for s in range(2):

        def source(i):
            row = (i + row_shift) & (PX - 1)
            return volume[pl.ds(s * CH * PX + row, CH, stride=PX), :]

        near = source(0)
        for i in range(PX):
            far = source(i + 1)
            row = (1.0 - f_row) * near + f_row * far
            near = far
            value = (1.0 - f_col) * pltpu.roll(row, roll_near, 1) + f_col * pltpu.roll(
                row, roll_far, 1
            )
            out[i // ROWS, s, i % ROWS] = value


def weights_kernel(cond, w_in, w_mid, w_out_t, lhs_in, lhs_mid, lhs_out, back_mid, back_out):
    half_in = 0.5 * w_in[...]
    high, low = split(half_in[:CH])
    high, low = high.astype(f32), low.astype(f32)
    bias = cond[0, 0] * half_in[CH : CH + 1]
    for c in range(1, COND):
        bias = bias + cond[0, c] * half_in[CH + c : CH + c + 1]
    rows = jnp.concatenate([high, high, low, *split3(bias), jnp.zeros((5, HID), f32)], 0)
    lhs_in[...] = rows.T.astype(bf16)

    half_mid = 0.5 * w_mid[...]
    high, low = split(half_mid.T)
    lhs_mid[:HID, :HID] = high
    lhs_mid[:HID, HID:] = high
    lhs_mid[HID:, :HID] = low
    lhs_mid[HID:, HID:] = low
    high, low = split(half_mid)
    back_mid[:HID, :HID] = high
    back_mid[:HID, HID:] = high
    back_mid[HID:, :HID] = low
    back_mid[HID:, HID:] = low

    out_t = w_out_t[...]
    high, low = split(out_t)
    high, low = high.astype(f32), low.astype(f32)
    pair = jnp.concatenate([high, low, jnp.zeros((8, HID), f32)], 0).astype(bf16)
    lhs_out[:, :HID] = pair
    lhs_out[:, HID:] = pair
    rows = 0.5 * jnp.concatenate([high, high, low, jnp.zeros((4, HID), f32)], 0)
    back_out[...] = rows.T.astype(bf16)


def activate(half):
    t = jnp.tanh(half)
    up = 1.0 + t
    value = half * up
    return value, up + value * (1.0 - t)


def softplus(x):
    z = jnp.exp(-jnp.abs(x))
    series = z * (1.0 - z * (0.5 - z * (1.0 / 3.0 - z * 0.25)))
    return jnp.maximum(x, 0.0) + jnp.where(z < 0.03, series, jnp.log(1.0 + z))


def one_minus_exp(x):
    terms = (1.0 / 2, 1.0 / 3, 1.0 / 4, 1.0 / 5, 1.0 / 6, 1.0 / 7)
    series = jnp.ones_like(x)
    for factor in reversed(terms):
        series = 1.0 - x * factor * series
    return jnp.where(x < 0.25, x * series, 1.0 - jnp.exp(-x))


def logistic(x):
    return 1.0 / (1.0 + jnp.exp(-x))


def render_kernel(
    offsets,
    order,
    cond,
    slices,
    cot,
    lhs_in,
    lhs_mid,
    lhs_out,
    back_mid,
    back_out,
    image,
    grads,
    feats,
    h1,
    d1,
    h2,
    d2,
    raw,
    graw,
    acc_mid,
    acc_in,
    acc_out,
):
    f_depth = offsets[0, 2]
    facing = order[0]

    def forward(k):
        f_next = jnp.where(k == NZ - 1, 0.0, f_depth)
        after = jnp.minimum(k + 1, NZ - 1)
        x = jnp.concatenate(
            [(1.0 - f_depth) * slices[k, r] + f_next * slices[after, r] for r in range(ROWS)], 1
        )
        high = x.astype(bf16).astype(f32)
        features = jnp.concatenate([high, x - high, high, jnp.ones_like(x)], 0).astype(bf16)
        feats[k] = features
        value, slope = activate(mul(lhs_in[...], features))
        high, low = split(value)
        d1[k] = slope
        h1[k, :HID] = high
        h1[k, HID:] = low
        pair = jnp.concatenate([high, low], 0)
        value, slope = activate(two_halves(mul(lhs_mid[...], pair)))
        high, low = split(value)
        d2[k] = slope
        h2[k, :HID] = high
        h2[k, HID:] = low
        pair = jnp.concatenate([high, low], 0)
        result = mul(lhs_out[...], pair)[:8]
        put(raw, pl.ds(pl.multiple_of(8 * k, 8), 8), result + pltpu.roll(result, 4, 0))

    def forward_some(i, carry):
        for u in range(UNROLL):
            forward(i * UNROLL + u)
        return carry

    lax.fori_loop(0, NZ // UNROLL, forward_some, 0)

    def strided(ref, o):
        return get(ref, pl.ds(o, NZ, stride=8))

    row = lax.broadcasted_iota(jnp.int32, (NZ, NZ), 0)
    column = lax.broadcasted_iota(jnp.int32, (NZ, NZ), 1)
    sign = 1 - 2 * facing
    earlier = jnp.where((row - column) * sign > 0, 1.0, 0.0)
    later = jnp.where((column - row) * sign > 0, 1.0, 0.0)

    def summed(mask, value):
        mask = jnp.concatenate([mask] * 3, 1).astype(bf16)
        return mul(mask, jnp.concatenate(split3(value), 0).astype(bf16))

    raw_sigma = strided(raw, 0)
    optical = STEP_DEPTH * softplus(raw_sigma)
    transmit = jnp.exp(-summed(earlier, optical))
    weight = transmit * one_minus_exp(optical)
    gain = jnp.zeros_like(weight)
    for c in range(3):
        rgb = logistic(strided(raw, c + 1))
        picture = jnp.sum(weight * rgb, 0, keepdims=True)
        for r in range(ROWS):
            image[c, r : r + 1, :] = picture[:, r * PY : (r + 1) * PY]
        cot_c = jnp.concatenate([cot[c, r : r + 1, :] for r in range(ROWS)], 1)
        gain = gain + cot_c * rgb
        put(graw, pl.ds(c + 1, NZ, stride=8), weight * cot_c * (rgb * (1.0 - rgb)))
    grad_optical = gain * transmit * jnp.exp(-optical) - summed(later, gain * weight)
    put(graw, pl.ds(0, NZ, stride=8), STEP_DEPTH * grad_optical * logistic(raw_sigma))

    acc_mid[...] = jnp.zeros_like(acc_mid)
    acc_in[...] = jnp.zeros_like(acc_in)
    acc_out[...] = jnp.zeros_like(acc_out)
    first = lax.broadcasted_iota(jnp.int32, (8, RAYS), 0) < 4

    def backward(k):
        g = get(graw, pl.ds(pl.multiple_of(8 * k, 8), 8))
        g = jnp.where(first, g, pltpu.roll(g, 4, 0))
        high = g.astype(bf16).astype(f32)
        pair = jnp.where(first, high, g - high)
        cotangent = jnp.concatenate([pair, jnp.where(first, high, 0.0)], 0).astype(bf16)
        delta = mul(back_out[...], cotangent) * d2[k]
        acc_out[...] += mul_t(cotangent, h2[k])
        pair = jnp.concatenate(split(delta), 0)
        acc_mid[...] += mul_t(h1[k], pair)
        delta = two_halves(mul(back_mid[...], pair)) * d1[k]
        pair = jnp.concatenate(split(delta), 0)
        acc_in[...] += mul_t(feats[k], pair)

    def backward_some(i, carry):
        for u in range(UNROLL):
            backward(i * UNROLL + u)
        return carry

    lax.fori_loop(0, NZ // UNROLL, backward_some, 0)

    grads[:HID] = two_sides(two_halves(acc_mid[...]))
    total = two_sides(acc_in[...])
    grads[HID : HID + CH] = total[:CH] + total[CH : 2 * CH]
    for c in range(COND):
        grads[HID + CH + c : HID + CH + c + 1] = cond[0, c] * total[3 * CH : 3 * CH + 1]
    total = two_sides(acc_out[...])[:8]
    used = HID + CH + COND
    grads[used : used + 8] = total + pltpu.roll(total, 4, 0)
    grads[used + 8 :] = jnp.zeros((grads.shape[0] - used - 8, HID), f32)


def sum_kernel(parts, out):
    total = parts[0]
    for i in range(1, PIECES):
        total = total + parts[i]
    for i in range(PIECES):
        out[i] = total


def unpack_kernel(packed, grad_in, grad_mid, grad_out_t):
    grad_mid[...] = packed[:HID]
    grad_in[...] = packed[HID : HID + CH + COND]
    grad_out_t[...] = packed[HID + CH + COND : HID + CH + COND + 4]


def shape(dims, dtype=f32):
    return jax.ShapeDtypeStruct(dims, dtype)


def exchange(parts, axes):
    return lax.all_to_all(parts, axes, 0, 0, tiled=True)


def per_device(volume, offsets, shifts, order, cond, w_in, w_mid, w_out, cot_image):
    rows = pl.pallas_call(
        resample_kernel,
        out_shape=shape((8, 2, ROWS, CH, PY)),
        in_specs=[SMEM, SMEM, VMEM],
        out_specs=VMEM,
    )(offsets, shifts, volume.reshape(2 * CH * PX, PY))
    slices = exchange(rows, BRICK).reshape(NZ, ROWS, CH, PY)
    weights = pl.pallas_call(
        weights_kernel,
        out_shape=(
            shape((HID, 32), bf16),
            shape((2 * HID, 2 * HID), bf16),
            shape((16, 2 * HID), bf16),
            shape((2 * HID, 2 * HID), bf16),
            shape((HID, 16), bf16),
        ),
        in_specs=[SMEM, VMEM, VMEM, VMEM],
        out_specs=(VMEM,) * 5,
    )(cond, w_in, w_mid, w_out.T)
    image, grads = pl.pallas_call(
        render_kernel,
        out_shape=(shape((3, ROWS, PY)), shape((PIECES * PIECE_ROWS, HID))),
        in_specs=[SMEM, SMEM, SMEM] + [VMEM] * 7,
        out_specs=(VMEM, VMEM),
        scratch_shapes=[
            pltpu.VMEM((NZ, 32, RAYS), bf16),
            pltpu.VMEM((NZ, 2 * HID, RAYS), bf16),
            pltpu.VMEM((NZ, HID, RAYS), f32),
            pltpu.VMEM((NZ, 2 * HID, RAYS), bf16),
            pltpu.VMEM((NZ, HID, RAYS), f32),
            pltpu.VMEM((ROWS, NZ * 8, PY), f32),
            pltpu.VMEM((ROWS, NZ * 8, PY), f32),
            pltpu.VMEM((2 * HID, 2 * HID), f32),
            pltpu.VMEM((32, 2 * HID), f32),
            pltpu.VMEM((16, 2 * HID), f32),
        ],
    )(offsets, order, cond, slices, cot_image[0], *weights)

    def total(parts):
        return pl.pallas_call(
            sum_kernel, out_shape=shape(parts.shape), in_specs=[VMEM], out_specs=VMEM
        )(parts)

    parts = grads.reshape(PIECES, PIECE_ROWS, HID)
    parts = total(exchange(parts, NEAR))
    parts = total(exchange(parts, FAR))
    packed = exchange(parts, NEAR).reshape(PIECES * PIECE_ROWS, HID)
    grad_in, grad_mid, grad_out_t = pl.pallas_call(
        unpack_kernel,
        out_shape=(shape((CH + COND, HID)), shape((HID, HID)), shape((4, HID))),
        in_specs=[VMEM],
        out_specs=(VMEM,) * 3,
    )(packed)
    return image[None], grad_in, grad_mid, grad_out_t.T


def solution(mesh):
    torus = Mesh(
        mesh.devices.reshape(2, 2, 8, 4, 2), ("y_far", "y_near", "z", "x", "core")
    )
    return jax.shard_map(
        per_device,
        mesh=torus,
        in_specs=(
            P(BRICK, None, None, None),
            P(VIEW, None),
            P(VIEW, None),
            P(VIEW),
            P(VIEW, None),
            P(),
            P(),
            P(),
            P(VIEW, None, BRICK, None),
        ),
        out_specs=(P(VIEW, None, BRICK, None), P(), P(), P()),
        check_vma=False,
    )
```

```python
import functools

import jax
import jax.numpy as jnp
from jax import lax
from jax.experimental import pallas as pl
from jax.experimental.pallas import tpu as pltpu
from jax.sharding import Mesh
from jax.sharding import PartitionSpec as P

VIEW = ("y_far", "y_near", "z")
BRICK = ("x", "core")
NEAR = ("y_near", "x", "core")
FAR = ("y_far", "z")

STEP_DEPTH = 0.15
NZ, CH, COND, HID = 16, 8, 8, 128
PX, PY = 32, 128
ROWS = 4
RAYS = ROWS * PY
PIECES, PIECE_ROWS = 16, 16

bf16, f32 = jnp.bfloat16, jnp.float32
VMEM = pl.BlockSpec(memory_space=pltpu.VMEM)
SMEM = pl.BlockSpec(memory_space=pltpu.SMEM)


def split(value):
    high = value.astype(bf16)
    return high, (value - high.astype(f32)).astype(bf16)


def split3(value):
    high = value.astype(bf16).astype(f32)
    rest = value - high
    middle = rest.astype(bf16).astype(f32)
    return high, middle, rest - middle


def mul(a, b):
    return jnp.dot(a, b, preferred_element_type=f32)


def mul_t(a, b):
    return lax.dot_general(a, b, (((1,), (1,)), ((), ())), preferred_element_type=f32)


def two_halves(value):
    return value[: value.shape[0] // 2] + value[value.shape[0] // 2 :]


def two_sides(value):
    return value[:, : value.shape[1] // 2] + value[:, value.shape[1] // 2 :]


def get(ref, rows):
    return jnp.concatenate([ref[r, rows, :] for r in range(ROWS)], 1)


def put(ref, rows, value):
    for r in range(ROWS):
        ref[r, rows, :] = value[:, r * PY : (r + 1) * PY]


def resample_kernel(offsets, shifts, volume, out):
    f_row, f_col = offsets[0, 0], offsets[0, 1]
    row_shift = shifts[0, 0] & (PX - 1)
    col_shift = shifts[0, 1] & (PY - 1)
    roll_near = (PY - col_shift) & (PY - 1)
    roll_far = (PY - 1 - col_shift) & (PY - 1)

    for s in range(2):

        def source(i):
            row = (i + row_shift) & (PX - 1)
            return volume[pl.ds(s * CH * PX + row, CH, stride=PX), :]

        near = source(0)
        for i in range(PX):
            far = source(i + 1)
            row = (1.0 - f_row) * near + f_row * far
            near = far
            value = (1.0 - f_col) * pltpu.roll(row, roll_near, 1) + f_col * pltpu.roll(
                row, roll_far, 1
            )
            out[i // ROWS, s, i % ROWS] = value


def prepare_kernel(
    offsets, order, cond, w_in, w_mid, w_out_t, cot_rows, per_ray, per_channel, masks, lhs_in, lhs_mid, lhs_out, back_mid, back_out
):
    half_in = 0.5 * w_in[...]
    high, low = split(half_in[:CH])
    high, low = high.astype(f32), low.astype(f32)
    bias = cond[0, 0] * half_in[CH : CH + 1]
    for c in range(1, COND):
        bias = bias + cond[0, c] * half_in[CH + c : CH + c + 1]
    rows = jnp.concatenate([high, high, low, *split3(bias), jnp.zeros((5, HID), f32)], 0)
    lhs_in[...] = rows.T.astype(bf16)

    half_mid = 0.5 * w_mid[...]
    high, low = split(half_mid.T)
    lhs_mid[:HID, :HID] = high
    lhs_mid[:HID, HID:] = high
    lhs_mid[HID:, :HID] = low
    lhs_mid[HID:, HID:] = low
    high, low = split(half_mid)
    back_mid[:HID, :HID] = high
    back_mid[:HID, HID:] = high
    back_mid[HID:, :HID] = low
    back_mid[HID:, HID:] = low

    out_t = w_out_t[...]
    high, low = split(out_t)
    high, low = high.astype(f32), low.astype(f32)
    pair = jnp.concatenate([high, low, jnp.zeros((8, HID), f32)], 0).astype(bf16)
    lhs_out[:, :HID] = pair
    lhs_out[:, HID:] = pair
    rows = 0.5 * jnp.concatenate([high, high, low, jnp.zeros((4, HID), f32)], 0)
    back_out[...] = rows.T.astype(bf16)

    for c in range(3):
        for r in range(ROWS):
            per_ray[c : c + 1, r * PY : (r + 1) * PY] = cot_rows[c, r : r + 1, :]
    per_ray[3:] = jnp.full((5, RAYS), offsets[0, 2], f32)
    for c in range(COND):
        per_channel[c : c + 1] = jnp.full((1, HID), cond[0, c], f32)

    row = lax.broadcasted_iota(jnp.int32, (2 * NZ, 3 * NZ), 0)
    column = lax.broadcasted_iota(jnp.int32, (2 * NZ, 3 * NZ), 1) & (NZ - 1)
    ahead = ((row & (NZ - 1)) - column) * (1 - 2 * order[0])
    ahead = jnp.where(row < NZ, ahead, -ahead)
    masks[...] = jnp.where(ahead > 0, 1.0, 0.0).astype(bf16)


def activate(half):
    up = 1.0 + jnp.tanh(half)
    return half * up, up


def slope_of(value, up):
    return up + value * (2.0 - up)


def softplus(x):
    z = jnp.exp(-jnp.abs(x))
    series = z * (1.0 - z * (0.5 - z * (1.0 / 3.0 - z * 0.25)))
    return jnp.maximum(x, 0.0) + jnp.where(z < 0.03, series, jnp.log(1.0 + z))


def one_minus_exp(x):
    terms = (1.0 / 2, 1.0 / 3, 1.0 / 4, 1.0 / 5, 1.0 / 6, 1.0 / 7)
    series = jnp.ones_like(x)
    for factor in reversed(terms):
        series = 1.0 - x * factor * series
    return jnp.where(x < 0.25, x * series, 1.0 - jnp.exp(-x))


def logistic(x):
    return 1.0 / (1.0 + jnp.exp(-x))


def render_kernel(
    slices,
    per_ray,
    per_channel,
    masks,
    lhs_in,
    lhs_mid,
    lhs_out,
    back_mid,
    back_out,
    image,
    grads,
    *scratch,
):
    raw, graw, acc_mid, acc_in, acc_out = scratch[-5:]
    feats, h1, h2, value1, up1, value2, up2 = zip(scratch[:7], scratch[7:14])
    delta2, delta1 = zip(scratch[14:16], scratch[16:18])

    def layer_in(i, p):
        k = 2 * i + p
        f_depth = per_ray[3:4, :PY]
        f_next = jnp.where(k == NZ - 1, 0.0, f_depth)
        after = jnp.minimum(k + 1, NZ - 1)
        x = jnp.concatenate(
            [(1.0 - f_depth) * slices[k, r] + f_next * slices[after, r] for r in range(ROWS)], 1
        )
        high = x.astype(bf16).astype(f32)
        features = jnp.concatenate([high, x - high, high, jnp.ones_like(x)], 0).astype(bf16)
        feats[p][i] = features
        value, up = activate(mul(lhs_in[...], features))
        value1[p][i] = value
        up1[p][i] = up
        h1[p][i, :HID], h1[p][i, HID:] = split(value)

    def layer_mid(i, p):
        value, up = activate(two_halves(mul(lhs_mid[...], h1[p][i])))
        value2[p][i] = value
        up2[p][i] = up
        h2[p][i, :HID], h2[p][i, HID:] = split(value)

    def layer_out(i, p):
        result = mul(lhs_out[...], h2[p][i])[:8]
        row = pl.multiple_of(16 * i + 8 * p, 8)
        put(raw, pl.ds(row, 8), result + pltpu.roll(result, 4, 0))

    pipeline(layer_in, layer_mid, layer_out)

    def strided(ref, o):
        return get(ref, pl.ds(o, NZ, stride=8))

    def summed(mask, value):
        return mul(mask, jnp.concatenate(split3(value), 0).astype(bf16))

    raw_sigma = strided(raw, 0)
    optical = STEP_DEPTH * softplus(raw_sigma)
    transmit = jnp.exp(-summed(masks[:NZ], optical))
    weight = transmit * one_minus_exp(optical)
    gain = jnp.zeros_like(weight)
    for c in range(3):
        rgb = logistic(strided(raw, c + 1))
        picture = jnp.sum(weight * rgb, 0, keepdims=True)
        for r in range(ROWS):
            image[c, r : r + 1, :] = picture[:, r * PY : (r + 1) * PY]
        cot_c = per_ray[c : c + 1, :]
        gain = gain + cot_c * rgb
        put(graw, pl.ds(c + 1, NZ, stride=8), weight * cot_c * (rgb * (1.0 - rgb)))
    grad_optical = gain * transmit * jnp.exp(-optical) - summed(masks[NZ:], gain * weight)
    put(graw, pl.ds(0, NZ, stride=8), STEP_DEPTH * grad_optical * logistic(raw_sigma))

    acc_mid[...] = jnp.zeros_like(acc_mid)
    acc_in[...] = jnp.zeros_like(acc_in)
    acc_out[...] = jnp.zeros_like(acc_out)
    first = lax.broadcasted_iota(jnp.int32, (8, RAYS), 0) < 4

    def back_from_out(i, p):
        g = get(graw, pl.ds(pl.multiple_of(16 * i + 8 * p, 8), 8))
        g = jnp.where(first, g, pltpu.roll(g, 4, 0))
        high = g.astype(bf16).astype(f32)
        pair = jnp.where(first, high, g - high)
        cotangent = jnp.concatenate([pair, jnp.where(first, high, 0.0)], 0).astype(bf16)
        delta2[p][...] = mul(back_out[...], cotangent) * slope_of(value2[p][i], up2[p][i])
        acc_out[...] += mul_t(cotangent, h2[p][i])

    def back_from_mid(i, p):
        pair = jnp.concatenate(split(delta2[p][...]), 0)
        acc_mid[...] += mul_t(h1[p][i], pair)
        delta1[p][...] = two_halves(mul(back_mid[...], pair)) * slope_of(value1[p][i], up1[p][i])

    def back_from_in(i, p):
        pair = jnp.concatenate(split(delta1[p][...]), 0)
        acc_in[...] += mul_t(feats[p][i], pair)

    pipeline(back_from_out, back_from_mid, back_from_in)

    grads[:HID] = two_sides(two_halves(acc_mid[...]))
    total = two_sides(acc_in[...])
    grads[HID : HID + CH] = total[:CH] + total[CH : 2 * CH]
    grads[HID + CH : HID + CH + COND] = per_channel[...] * total[3 * CH : 3 * CH + 1]
    total = two_sides(acc_out[...])[:8]
    used = HID + CH + COND
    grads[used : used + 8] = total + pltpu.roll(total, 4, 0)
    grads[used + 8 :] = jnp.zeros((grads.shape[0] - used - 8, HID), f32)


def pipeline(first, second, third):
    def step(i, carry):
        third(i - 1, 0)
        second(i - 1, 1)
        first(i, 0)
        third(i - 1, 1)
        second(i, 0)
        first(i, 1)
        return carry

    first(0, 0)
    second(0, 0)
    first(0, 1)
    lax.fori_loop(1, NZ // 2, step, 0)
    last = NZ // 2 - 1
    third(last, 0)
    second(last, 1)
    third(last, 1)


def sum_kernel(parts, out):
    total = parts[0]
    for i in range(1, PIECES):
        total = total + parts[i]
    for i in range(PIECES):
        out[i] = total


def unpack_kernel(packed, grad_in, grad_mid, grad_out_t):
    grad_mid[...] = packed[:HID]
    grad_in[...] = packed[HID : HID + CH + COND]
    grad_out_t[...] = packed[HID + CH + COND : HID + CH + COND + 4]


def room(mebibytes):
    return pltpu.CompilerParams(vmem_limit_bytes=mebibytes * 2**20)


def shape(dims, dtype=f32):
    return jax.ShapeDtypeStruct(dims, dtype)


def exchange(parts, axes):
    return lax.all_to_all(parts, axes, 0, 0, tiled=True)


def per_device(volume, offsets, shifts, order, cond, w_in, w_mid, w_out, cot_image):
    rows = pl.pallas_call(
        resample_kernel,
        out_shape=shape((8, 2, ROWS, CH, PY)),
        in_specs=[SMEM, SMEM, VMEM],
        out_specs=VMEM,
    )(offsets, shifts, volume.reshape(2 * CH * PX, PY))
    slices = exchange(rows, BRICK).reshape(NZ, ROWS, CH, PY)
    prepared = pl.pallas_call(
        prepare_kernel,
        out_shape=(
            shape((8, RAYS)),
            shape((COND, HID)),
            shape((2 * NZ, 3 * NZ), bf16),
            shape((HID, 32), bf16),
            shape((2 * HID, 2 * HID), bf16),
            shape((16, 2 * HID), bf16),
            shape((2 * HID, 2 * HID), bf16),
            shape((HID, 16), bf16),
        ),
        in_specs=[SMEM] * 3 + [VMEM] * 4,
        out_specs=(VMEM,) * 8,
        compiler_params=room(2),
    )(offsets, order, cond, w_in, w_mid, w_out.T, cot_image[0])
    half = NZ // 2
    slabs = [
        pltpu.VMEM((half, 32, RAYS), bf16),
        pltpu.VMEM((half, 2 * HID, RAYS), bf16),
        pltpu.VMEM((half, 2 * HID, RAYS), bf16),
        *[pltpu.VMEM((half, HID, RAYS), f32)] * 4,
    ]
    image, grads = pl.pallas_call(
        render_kernel,
        out_shape=(shape((3, ROWS, PY)), shape((PIECES * PIECE_ROWS, HID))),
        in_specs=[VMEM] * 9,
        out_specs=(VMEM, VMEM),
        scratch_shapes=[
            *slabs,
            *slabs,
            *[pltpu.VMEM((HID, RAYS), f32)] * 4,
            pltpu.VMEM((ROWS, NZ * 8, PY), f32),
            pltpu.VMEM((ROWS, NZ * 8, PY), f32),
            pltpu.VMEM((2 * HID, 2 * HID), f32),
            pltpu.VMEM((32, 2 * HID), f32),
            pltpu.VMEM((16, 2 * HID), f32),
        ],
        compiler_params=room(34),
    )(slices, *prepared)

    def total(parts):
        return pl.pallas_call(
            sum_kernel,
            out_shape=shape(parts.shape),
            in_specs=[VMEM],
            out_specs=VMEM,
            compiler_params=room(2),
        )(parts)

    parts = grads.reshape(PIECES, PIECE_ROWS, HID)
    parts = total(exchange(parts, NEAR))
    parts = total(exchange(parts, FAR))
    packed = exchange(parts, NEAR).reshape(PIECES * PIECE_ROWS, HID)
    grad_in, grad_mid, grad_out_t = pl.pallas_call(
        unpack_kernel,
        out_shape=(shape((CH + COND, HID)), shape((HID, HID)), shape((4, HID))),
        in_specs=[VMEM],
        out_specs=(VMEM,) * 3,
        compiler_params=room(2),
    )(packed)
    return image[None], grad_in, grad_mid, grad_out_t.T


def solution(mesh):
    torus = Mesh(
        mesh.devices.reshape(2, 2, 8, 4, 2), ("y_far", "y_near", "z", "x", "core")
    )
    return jax.shard_map(
        per_device,
        mesh=torus,
        in_specs=(
            P(BRICK, None, None, None),
            P(VIEW, None),
            P(VIEW, None),
            P(VIEW),
            P(VIEW, None),
            P(),
            P(),
            P(),
            P(VIEW, None, BRICK, None),
        ),
        out_specs=(P(VIEW, None, BRICK, None), P(), P(), P()),
        check_vma=False,
    )
```

```python
import functools

import jax
import jax.numpy as jnp
from jax import lax
from jax.experimental import pallas as pl
from jax.experimental.pallas import tpu as pltpu
from jax.sharding import Mesh
from jax.sharding import PartitionSpec as P

VIEW = ("y_far", "y_near", "z")
BRICK = ("x", "core")
NEAR = ("y_near", "x", "core")
FAR = ("y_far", "z")

STEP_DEPTH = 0.15
NZ, CH, COND, HID = 16, 8, 8, 128
PX, PY = 32, 128
ROWS = 4
RAYS = ROWS * PY
PIECES, TILES = 16, 10

bf16, f32 = jnp.bfloat16, jnp.float32
VMEM = pl.BlockSpec(memory_space=pltpu.VMEM)
SMEM = pl.BlockSpec(memory_space=pltpu.SMEM)


def split(value):
    high = value.astype(bf16)
    return high, (value - high.astype(f32)).astype(bf16)


def split3(value):
    high = value.astype(bf16).astype(f32)
    rest = value - high
    middle = rest.astype(bf16).astype(f32)
    return high, middle, rest - middle


def mul(a, b):
    return jnp.dot(a, b, preferred_element_type=f32)


def mul_t(a, b):
    return lax.dot_general(a, b, (((1,), (1,)), ((), ())), preferred_element_type=f32)


def two_halves(value):
    return value[: value.shape[0] // 2] + value[value.shape[0] // 2 :]


def two_sides(value):
    return value[:, : value.shape[1] // 2] + value[:, value.shape[1] // 2 :]


def get(ref, rows):
    return jnp.concatenate([ref[r, rows, :] for r in range(ROWS)], 1)


def put(ref, rows, value):
    for r in range(ROWS):
        ref[r, rows, :] = value[:, r * PY : (r + 1) * PY]


def resample_kernel(offsets, shifts, volume, out):
    f_row, f_col = offsets[0, 0], offsets[0, 1]
    row_shift = shifts[0, 0] & (PX - 1)
    col_shift = shifts[0, 1] & (PY - 1)
    roll_near = (PY - col_shift) & (PY - 1)
    roll_far = (PY - 1 - col_shift) & (PY - 1)

    for s in range(2):

        def source(i):
            row = (i + row_shift) & (PX - 1)
            return volume[pl.ds(s * CH * PX + row, CH, stride=PX), :]

        near = source(0)
        for i in range(PX):
            far = source(i + 1)
            row = (1.0 - f_row) * near + f_row * far
            near = far
            value = (1.0 - f_col) * pltpu.roll(row, roll_near, 1) + f_col * pltpu.roll(
                row, roll_far, 1
            )
            out[i // ROWS, s, i % ROWS] = value


def prepare_kernel(
    offsets, order, cond, w_in, w_mid, w_out_t, cot_rows, per_ray, per_channel, masks, lhs_in, lhs_mid, lhs_out, back_mid, back_out
):
    half_in = 0.5 * w_in[...]
    high, low = split(half_in[:CH])
    high, low = high.astype(f32), low.astype(f32)
    bias = cond[0, 0] * half_in[CH : CH + 1]
    for c in range(1, COND):
        bias = bias + cond[0, c] * half_in[CH + c : CH + c + 1]
    rows = jnp.concatenate([high, high, low, *split3(bias), jnp.zeros((5, HID), f32)], 0)
    lhs_in[...] = rows.T.astype(bf16)

    half_mid = 0.5 * w_mid[...]
    high, low = split(half_mid.T)
    lhs_mid[:HID, :HID] = high
    lhs_mid[:HID, HID:] = high
    lhs_mid[HID:, :HID] = low
    lhs_mid[HID:, HID:] = low
    high, low = split(half_mid)
    back_mid[:HID, :HID] = high
    back_mid[:HID, HID:] = high
    back_mid[HID:, :HID] = low
    back_mid[HID:, HID:] = low

    out_t = w_out_t[...]
    high, low = split(out_t)
    high, low = high.astype(f32), low.astype(f32)
    pair = jnp.concatenate([high, low, jnp.zeros((8, HID), f32)], 0).astype(bf16)
    lhs_out[:, :HID] = pair
    lhs_out[:, HID:] = pair
    rows = 0.5 * jnp.concatenate([high, high, low, jnp.zeros((4, HID), f32)], 0)
    back_out[...] = rows.T.astype(bf16)

    for c in range(3):
        for r in range(ROWS):
            per_ray[c : c + 1, r * PY : (r + 1) * PY] = cot_rows[c, r : r + 1, :]
    per_ray[3:] = jnp.full((5, RAYS), offsets[0, 2], f32)
    for c in range(COND):
        per_channel[c : c + 1] = jnp.full((1, HID), cond[0, c], f32)

    row = lax.broadcasted_iota(jnp.int32, (2 * NZ, 3 * NZ), 0)
    column = lax.broadcasted_iota(jnp.int32, (2 * NZ, 3 * NZ), 1) & (NZ - 1)
    ahead = ((row & (NZ - 1)) - column) * (1 - 2 * order[0])
    ahead = jnp.where(row < NZ, ahead, -ahead)
    masks[...] = jnp.where(ahead > 0, 1.0, 0.0).astype(bf16)


def activate(half):
    up = 1.0 + jnp.tanh(half)
    return half * up, up


def slope_of(value, up):
    return up + value * (2.0 - up)


def softplus(x):
    z = jnp.exp(-jnp.abs(x))
    series = z * (1.0 - z * (0.5 - z * (1.0 / 3.0 - z * 0.25)))
    return jnp.maximum(x, 0.0) + jnp.where(z < 0.03, series, jnp.log(1.0 + z))


def one_minus_exp(x):
    terms = (1.0 / 2, 1.0 / 3, 1.0 / 4, 1.0 / 5, 1.0 / 6, 1.0 / 7)
    series = jnp.ones_like(x)
    for factor in reversed(terms):
        series = 1.0 - x * factor * series
    return jnp.where(x < 0.25, x * series, 1.0 - jnp.exp(-x))


def logistic(x):
    return 1.0 / (1.0 + jnp.exp(-x))


def render_kernel(
    slices,
    per_ray,
    per_channel,
    masks,
    lhs_in,
    lhs_mid,
    lhs_out,
    back_mid,
    back_out,
    image,
    grads,
    *scratch,
):
    raw, graw, acc_mid, acc_in, acc_out = scratch[-5:]
    feats, h1, h2, value1, up1, value2, up2 = zip(scratch[:7], scratch[7:14])
    delta2, delta1 = zip(scratch[14:16], scratch[16:18])

    def layer_in(i, p):
        k = 2 * i + p
        f_depth = per_ray[3:4, :PY]
        f_next = jnp.where(k == NZ - 1, 0.0, f_depth)
        after = jnp.minimum(k + 1, NZ - 1)
        x = jnp.concatenate(
            [(1.0 - f_depth) * slices[k, r] + f_next * slices[after, r] for r in range(ROWS)], 1
        )
        high = x.astype(bf16).astype(f32)
        features = jnp.concatenate([high, x - high, high, jnp.ones_like(x)], 0).astype(bf16)
        feats[p][i] = features
        value, up = activate(mul(lhs_in[...], features))
        value1[p][i] = value
        up1[p][i] = up
        h1[p][i, :HID], h1[p][i, HID:] = split(value)

    def layer_mid(i, p):
        value, up = activate(two_halves(mul(lhs_mid[...], h1[p][i])))
        value2[p][i] = value
        up2[p][i] = up
        h2[p][i, :HID], h2[p][i, HID:] = split(value)

    def layer_out(i, p):
        result = mul(lhs_out[...], h2[p][i])[:8]
        row = pl.multiple_of(16 * i + 8 * p, 8)
        put(raw, pl.ds(row, 8), result + pltpu.roll(result, 4, 0))

    pipeline(layer_in, layer_mid, layer_out)

    def strided(ref, o):
        return get(ref, pl.ds(o, NZ, stride=8))

    def summed(mask, value):
        return mul(mask, jnp.concatenate(split3(value), 0).astype(bf16))

    raw_sigma = strided(raw, 0)
    optical = STEP_DEPTH * softplus(raw_sigma)
    transmit = jnp.exp(-summed(masks[:NZ], optical))
    weight = transmit * one_minus_exp(optical)
    gain = jnp.zeros_like(weight)
    for c in range(3):
        rgb = logistic(strided(raw, c + 1))
        picture = jnp.sum(weight * rgb, 0, keepdims=True)
        for r in range(ROWS):
            image[c, r : r + 1, :] = picture[:, r * PY : (r + 1) * PY]
        cot_c = per_ray[c : c + 1, :]
        gain = gain + cot_c * rgb
        put(graw, pl.ds(c + 1, NZ, stride=8), weight * cot_c * (rgb * (1.0 - rgb)))
    grad_optical = gain * transmit * jnp.exp(-optical) - summed(masks[NZ:], gain * weight)
    put(graw, pl.ds(0, NZ, stride=8), STEP_DEPTH * grad_optical * logistic(raw_sigma))

    acc_mid[...] = jnp.zeros_like(acc_mid)
    acc_in[...] = jnp.zeros_like(acc_in)
    acc_out[...] = jnp.zeros_like(acc_out)
    first = lax.broadcasted_iota(jnp.int32, (8, RAYS), 0) < 4

    def back_from_out(i, p):
        g = get(graw, pl.ds(pl.multiple_of(16 * i + 8 * p, 8), 8))
        g = jnp.where(first, g, pltpu.roll(g, 4, 0))
        high = g.astype(bf16).astype(f32)
        pair = jnp.where(first, high, g - high)
        cotangent = jnp.concatenate([pair, jnp.where(first, high, 0.0)], 0).astype(bf16)
        delta2[p][...] = mul(back_out[...], cotangent) * slope_of(value2[p][i], up2[p][i])
        acc_out[...] += mul_t(cotangent, h2[p][i])

    def back_from_mid(i, p):
        pair = jnp.concatenate(split(delta2[p][...]), 0)
        acc_mid[...] += mul_t(h1[p][i], pair)
        delta1[p][...] = two_halves(mul(back_mid[...], pair)) * slope_of(value1[p][i], up1[p][i])

    def back_from_in(i, p):
        pair = jnp.concatenate(split(delta1[p][...]), 0)
        acc_in[...] += mul_t(feats[p][i], pair)

    pipeline(back_from_out, back_from_mid, back_from_in)

    total = two_sides(acc_in[...])
    rows_in = total[:CH] + total[CH : 2 * CH]
    rows_cond = per_channel[...] * total[3 * CH : 3 * CH + 1]
    total = two_sides(acc_out[...])[:8]
    rows_out = total + pltpu.roll(total, 4, 0)
    packed = jnp.concatenate(
        [
            two_sides(two_halves(acc_mid[...])),
            rows_in,
            rows_cond,
            rows_out,
            jnp.zeros((8, HID), f32),
        ],
        0,
    )
    for t in range(TILES):
        grads[:, 0, t * HID : (t + 1) * HID] = packed[t * PIECES : (t + 1) * PIECES]


def pipeline(first, second, third):
    def step(i, carry):
        for p in range(2):
            third(i - 2, p)
        for p in range(2):
            second(i - 1, p)
        for p in range(2):
            first(i, p)
        return carry

    both = range(2)
    last = NZ // 2 - 1
    [first(0, p) for p in both]
    [second(0, p) for p in both]
    [first(1, p) for p in both]
    lax.fori_loop(2, NZ // 2, step, 0)
    [third(last - 1, p) for p in both]
    [second(last, p) for p in both]
    [third(last, p) for p in both]


def sum_kernel(parts, out):
    total = parts[0]
    for i in range(1, PIECES):
        total = total + parts[i]
    for i in range(PIECES):
        out[i] = total


def unpack_kernel(packed, grad_in, grad_mid, grad_out_t):
    def rows(t):
        return packed[:, 0, t * HID : (t + 1) * HID]

    for t in range(HID // PIECES):
        grad_mid[t * PIECES : (t + 1) * PIECES] = rows(t)
    grad_in[...] = rows(HID // PIECES)
    grad_out_t[...] = rows(HID // PIECES + 1)[:4]


def room(mebibytes):
    return pltpu.CompilerParams(vmem_limit_bytes=mebibytes * 2**20)


def shape(dims, dtype=f32):
    return jax.ShapeDtypeStruct(dims, dtype)


def exchange(parts, axes):
    return lax.all_to_all(parts, axes, 0, 0, tiled=True)


def per_device(volume, offsets, shifts, order, cond, w_in, w_mid, w_out, cot_image):
    rows = pl.pallas_call(
        resample_kernel,
        out_shape=shape((8, 2, ROWS, CH, PY)),
        in_specs=[SMEM, SMEM, VMEM],
        out_specs=VMEM,
    )(offsets, shifts, volume.reshape(2 * CH * PX, PY))
    slices = exchange(rows, BRICK).reshape(NZ, ROWS, CH, PY)
    prepared = pl.pallas_call(
        prepare_kernel,
        out_shape=(
            shape((8, RAYS)),
            shape((COND, HID)),
            shape((2 * NZ, 3 * NZ), bf16),
            shape((HID, 32), bf16),
            shape((2 * HID, 2 * HID), bf16),
            shape((16, 2 * HID), bf16),
            shape((2 * HID, 2 * HID), bf16),
            shape((HID, 16), bf16),
        ),
        in_specs=[SMEM] * 3 + [VMEM] * 4,
        out_specs=(VMEM,) * 8,
        compiler_params=room(2),
    )(offsets, order, cond, w_in, w_mid, w_out.T, cot_image[0])
    half = NZ // 2
    slabs = [
        pltpu.VMEM((half, 32, RAYS), bf16),
        pltpu.VMEM((half, 2 * HID, RAYS), bf16),
        pltpu.VMEM((half, 2 * HID, RAYS), bf16),
        *[pltpu.VMEM((half, HID, RAYS), f32)] * 4,
    ]
    image, grads = pl.pallas_call(
        render_kernel,
        out_shape=(shape((3, ROWS, PY)), shape((PIECES, 1, TILES * HID))),
        in_specs=[VMEM] * 9,
        out_specs=(VMEM, VMEM),
        scratch_shapes=[
            *slabs,
            *slabs,
            *[pltpu.VMEM((HID, RAYS), f32)] * 4,
            pltpu.VMEM((ROWS, NZ * 8, PY), f32),
            pltpu.VMEM((ROWS, NZ * 8, PY), f32),
            pltpu.VMEM((2 * HID, 2 * HID), f32),
            pltpu.VMEM((32, 2 * HID), f32),
            pltpu.VMEM((16, 2 * HID), f32),
        ],
        compiler_params=pltpu.CompilerParams(
            vmem_limit_bytes=34 * 2**20
        ),
    )(slices, *prepared)

    def total(parts):
        return pl.pallas_call(
            sum_kernel,
            out_shape=shape(parts.shape),
            in_specs=[VMEM],
            out_specs=VMEM,
            compiler_params=room(2),
        )(parts)

    parts = total(exchange(grads, NEAR))
    parts = total(exchange(parts, FAR))
    packed = exchange(parts, NEAR)
    grad_in, grad_mid, grad_out_t = pl.pallas_call(
        unpack_kernel,
        out_shape=(shape((CH + COND, HID)), shape((HID, HID)), shape((4, HID))),
        in_specs=[VMEM],
        out_specs=(VMEM,) * 3,
        compiler_params=room(2),
    )(packed)
    return image[None], grad_in, grad_mid, grad_out_t.T


def solution(mesh):
    torus = Mesh(
        mesh.devices.reshape(2, 2, 8, 4, 2), ("y_far", "y_near", "z", "x", "core")
    )
    return jax.shard_map(
        per_device,
        mesh=torus,
        in_specs=(
            P(BRICK, None, None, None),
            P(VIEW, None),
            P(VIEW, None),
            P(VIEW),
            P(VIEW, None),
            P(),
            P(),
            P(),
            P(VIEW, None, BRICK, None),
        ),
        out_specs=(P(VIEW, None, BRICK, None), P(), P(), P()),
        check_vma=False,
    )
```

```python
import functools

import jax
import jax.numpy as jnp
from jax import lax
from jax.experimental import pallas as pl
from jax.experimental.pallas import tpu as pltpu
from jax.sharding import Mesh
from jax.sharding import PartitionSpec as P

VIEW = ("y_far", "y_near", "z")
BRICK = ("x", "core")
NEAR = ("y_near", "x", "core")
FAR = ("y_far", "z")

STEP_DEPTH = 0.15
NZ, CH, COND, HID = 16, 8, 8, 128
PX, PY = 32, 128
ROWS = 4
RAYS = ROWS * PY
PIECES, TILES = 16, 10
GROUP = 4

bf16, f32 = jnp.bfloat16, jnp.float32
VMEM = pl.BlockSpec(memory_space=pltpu.VMEM)
SMEM = pl.BlockSpec(memory_space=pltpu.SMEM)


def split(value):
    high = value.astype(bf16)
    return high, (value - high.astype(f32)).astype(bf16)


def split3(value):
    high = value.astype(bf16).astype(f32)
    rest = value - high
    middle = rest.astype(bf16).astype(f32)
    return high, middle, rest - middle


def mul(a, b):
    return jnp.dot(a, b, preferred_element_type=f32)


def mul_t(a, b):
    return lax.dot_general(a, b, (((1,), (1,)), ((), ())), preferred_element_type=f32)


def two_halves(value):
    return value[: value.shape[0] // 2] + value[value.shape[0] // 2 :]


def two_sides(value):
    return value[:, : value.shape[1] // 2] + value[:, value.shape[1] // 2 :]


def get(ref, rows):
    return jnp.concatenate([ref[r, rows, :] for r in range(ROWS)], 1)


def put(ref, rows, value):
    for r in range(ROWS):
        ref[r, rows, :] = value[:, r * PY : (r + 1) * PY]


def resample_kernel(offsets, shifts, volume, out):
    f_row, f_col = offsets[0, 0], offsets[0, 1]
    row_shift = shifts[0, 0] & (PX - 1)
    col_shift = shifts[0, 1] & (PY - 1)
    roll_near = (PY - col_shift) & (PY - 1)
    roll_far = (PY - 1 - col_shift) & (PY - 1)

    for s in range(2):

        def source(i):
            row = (i + row_shift) & (PX - 1)
            return volume[pl.ds(s * CH * PX + row, CH, stride=PX), :]

        near = source(0)
        for i in range(PX):
            far = source(i + 1)
            row = (1.0 - f_row) * near + f_row * far
            near = far
            value = (1.0 - f_col) * pltpu.roll(row, roll_near, 1) + f_col * pltpu.roll(
                row, roll_far, 1
            )
            out[i // ROWS, s, i % ROWS] = value


def prepare_kernel(
    offsets, order, cond, w_in, w_mid, w_out_t, cot_rows, per_ray, per_channel, masks, lhs_in, lhs_mid, lhs_out, back_mid, back_out
):
    half_in = 0.5 * w_in[...]
    high, low = split(half_in[:CH])
    high, low = high.astype(f32), low.astype(f32)
    bias = cond[0, 0] * half_in[CH : CH + 1]
    for c in range(1, COND):
        bias = bias + cond[0, c] * half_in[CH + c : CH + c + 1]
    rows = jnp.concatenate([high, high, low, *split3(bias), jnp.zeros((5, HID), f32)], 0)
    lhs_in[...] = rows.T.astype(bf16)

    half_mid = 0.5 * w_mid[...]
    high, low = split(half_mid.T)
    lhs_mid[:HID, :HID] = high
    lhs_mid[:HID, HID:] = high
    lhs_mid[HID:, :HID] = low
    lhs_mid[HID:, HID:] = low
    high, low = split(half_mid)
    back_mid[:HID, :HID] = high
    back_mid[:HID, HID:] = high
    back_mid[HID:, :HID] = low
    back_mid[HID:, HID:] = low

    out_t = w_out_t[...]
    high, low = split(out_t)
    high, low = high.astype(f32), low.astype(f32)
    pair = jnp.concatenate([high, low, jnp.zeros((8, HID), f32)], 0).astype(bf16)
    lhs_out[:, :HID] = pair
    lhs_out[:, HID:] = pair
    rows = 0.5 * jnp.concatenate([high, high, low, jnp.zeros((4, HID), f32)], 0)
    back_out[...] = rows.T.astype(bf16)

    for c in range(3):
        for r in range(ROWS):
            per_ray[c : c + 1, r * PY : (r + 1) * PY] = cot_rows[c, r : r + 1, :]
    per_ray[3:] = jnp.full((5, RAYS), offsets[0, 2], f32)
    for c in range(COND):
        per_channel[c : c + 1] = jnp.full((1, HID), cond[0, c], f32)

    row = lax.broadcasted_iota(jnp.int32, (2 * NZ, 3 * NZ), 0)
    column = lax.broadcasted_iota(jnp.int32, (2 * NZ, 3 * NZ), 1) & (NZ - 1)
    ahead = ((row & (NZ - 1)) - column) * (1 - 2 * order[0])
    ahead = jnp.where(row < NZ, ahead, -ahead)
    masks[...] = jnp.where(ahead > 0, 1.0, 0.0).astype(bf16)


def activate(half):
    up = 1.0 + jnp.tanh(half)
    return half * up, up


def slope_of(value, up):
    return up + value * (2.0 - up)


def softplus(x):
    z = jnp.exp(-jnp.abs(x))
    series = z * (1.0 - z * (0.5 - z * (1.0 / 3.0 - z * 0.25)))
    return jnp.maximum(x, 0.0) + jnp.where(z < 0.03, series, jnp.log(1.0 + z))


def one_minus_exp(x):
    terms = (1.0 / 2, 1.0 / 3, 1.0 / 4, 1.0 / 5, 1.0 / 6, 1.0 / 7)
    series = jnp.ones_like(x)
    for factor in reversed(terms):
        series = 1.0 - x * factor * series
    return jnp.where(x < 0.25, x * series, 1.0 - jnp.exp(-x))


def logistic(x):
    return 1.0 / (1.0 + jnp.exp(-x))


def render_kernel(
    slices,
    per_ray,
    per_channel,
    masks,
    lhs_in,
    lhs_mid,
    lhs_out,
    back_mid,
    back_out,
    image,
    grads,
    *scratch,
):
    raw, graw, acc_mid, acc_in, acc_out = scratch[-5:]
    sets = [scratch[9 * p : 9 * p + 9] for p in range(GROUP)]
    feats, h1, h2, value1, up1, value2, up2, delta2, delta1 = zip(*sets)

    def layer_in(i, p):
        k = GROUP * i + p
        f_depth = per_ray[3:4, :PY]
        f_next = jnp.where(k == NZ - 1, 0.0, f_depth)
        after = jnp.minimum(k + 1, NZ - 1)
        x = jnp.concatenate(
            [(1.0 - f_depth) * slices[k, r] + f_next * slices[after, r] for r in range(ROWS)], 1
        )
        high = x.astype(bf16).astype(f32)
        features = jnp.concatenate([high, x - high, high, jnp.ones_like(x)], 0).astype(bf16)
        feats[p][i] = features
        value, up = activate(mul(lhs_in[...], features))
        value1[p][i] = value
        up1[p][i] = up
        h1[p][i, :HID], h1[p][i, HID:] = split(value)

    def layer_mid(i, p):
        value, up = activate(two_halves(mul(lhs_mid[...], h1[p][i])))
        value2[p][i] = value
        up2[p][i] = up
        h2[p][i, :HID], h2[p][i, HID:] = split(value)

    def layer_out(i, p):
        result = mul(lhs_out[...], h2[p][i])[:8]
        row = pl.multiple_of(8 * GROUP * i + 8 * p, 8)
        put(raw, pl.ds(row, 8), result + pltpu.roll(result, 4, 0))

    pipeline(layer_in, layer_mid, layer_out)

    def strided(ref, o):
        return get(ref, pl.ds(o, NZ, stride=8))

    def summed(mask, value):
        return mul(mask, jnp.concatenate(split3(value), 0).astype(bf16))

    raw_sigma = strided(raw, 0)
    optical = STEP_DEPTH * softplus(raw_sigma)
    transmit = jnp.exp(-summed(masks[:NZ], optical))
    weight = transmit * one_minus_exp(optical)
    gain = jnp.zeros_like(weight)
    for c in range(3):
        rgb = logistic(strided(raw, c + 1))
        picture = jnp.sum(weight * rgb, 0, keepdims=True)
        for r in range(ROWS):
            image[c, r : r + 1, :] = picture[:, r * PY : (r + 1) * PY]
        cot_c = per_ray[c : c + 1, :]
        gain = gain + cot_c * rgb
        put(graw, pl.ds(c + 1, NZ, stride=8), weight * cot_c * (rgb * (1.0 - rgb)))
    grad_optical = gain * transmit * jnp.exp(-optical) - summed(masks[NZ:], gain * weight)
    put(graw, pl.ds(0, NZ, stride=8), STEP_DEPTH * grad_optical * logistic(raw_sigma))

    acc_mid[...] = jnp.zeros_like(acc_mid)
    acc_in[...] = jnp.zeros_like(acc_in)
    acc_out[...] = jnp.zeros_like(acc_out)
    first = lax.broadcasted_iota(jnp.int32, (8, RAYS), 0) < 4

    def back_from_out(i, p):
        g = get(graw, pl.ds(pl.multiple_of(8 * GROUP * i + 8 * p, 8), 8))
        g = jnp.where(first, g, pltpu.roll(g, 4, 0))
        high = g.astype(bf16).astype(f32)
        pair = jnp.where(first, high, g - high)
        cotangent = jnp.concatenate([pair, jnp.where(first, high, 0.0)], 0).astype(bf16)
        delta2[p][...] = mul(back_out[...], cotangent) * slope_of(value2[p][i], up2[p][i])
        acc_out[...] += mul_t(cotangent, h2[p][i])

    def back_from_mid(i, p):
        pair = jnp.concatenate(split(delta2[p][...]), 0)
        acc_mid[...] += mul_t(h1[p][i], pair)
        delta1[p][...] = two_halves(mul(back_mid[...], pair)) * slope_of(value1[p][i], up1[p][i])

    def back_from_in(i, p):
        pair = jnp.concatenate(split(delta1[p][...]), 0)
        acc_in[...] += mul_t(pair, feats[p][i])

    pipeline(back_from_out, back_from_mid, back_from_in)

    total = two_halves(acc_in[...]).T
    rows_in = total[:CH] + total[CH : 2 * CH]
    rows_cond = per_channel[...] * total[3 * CH : 3 * CH + 1]
    total = two_sides(acc_out[...])[:8]
    rows_out = total + pltpu.roll(total, 4, 0)
    packed = jnp.concatenate(
        [
            two_sides(two_halves(acc_mid[...])),
            rows_in,
            rows_cond,
            rows_out,
            jnp.zeros((8, HID), f32),
        ],
        0,
    )
    for t in range(TILES):
        grads[:, 0, t * HID : (t + 1) * HID] = packed[t * PIECES : (t + 1) * PIECES]


def pipeline(first, second, third):
    def step(i, carry):
        for p in group:
            third(i - 2, p)
        for p in group:
            second(i - 1, p)
        for p in group:
            first(i, p)
        return carry

    group = range(GROUP)
    last = NZ // GROUP - 1
    [first(0, p) for p in group]
    [second(0, p) for p in group]
    [first(1, p) for p in group]
    lax.fori_loop(2, last + 1, step, 0)
    [third(last - 1, p) for p in group]
    [second(last, p) for p in group]
    [third(last, p) for p in group]


def sum_kernel(parts, out):
    total = parts[0]
    for i in range(1, PIECES):
        total = total + parts[i]
    for i in range(PIECES):
        out[i] = total


def unpack_kernel(packed, grad_in, grad_mid, grad_out_t):
    def rows(t):
        return packed[:, 0, t * HID : (t + 1) * HID]

    for t in range(HID // PIECES):
        grad_mid[t * PIECES : (t + 1) * PIECES] = rows(t)
    grad_in[...] = rows(HID // PIECES)
    grad_out_t[...] = rows(HID // PIECES + 1)[:4]


def room(mebibytes):
    return pltpu.CompilerParams(vmem_limit_bytes=mebibytes * 2**20)


def shape(dims, dtype=f32):
    return jax.ShapeDtypeStruct(dims, dtype)


def exchange(parts, axes):
    return lax.all_to_all(parts, axes, 0, 0, tiled=True)


def per_device(volume, offsets, shifts, order, cond, w_in, w_mid, w_out, cot_image):
    rows = pl.pallas_call(
        resample_kernel,
        out_shape=shape((8, 2, ROWS, CH, PY)),
        in_specs=[SMEM, SMEM, VMEM],
        out_specs=VMEM,
    )(offsets, shifts, volume.reshape(2 * CH * PX, PY))
    slices = exchange(rows, BRICK).reshape(NZ, ROWS, CH, PY)
    prepared = pl.pallas_call(
        prepare_kernel,
        out_shape=(
            shape((8, RAYS)),
            shape((COND, HID)),
            shape((2 * NZ, 3 * NZ), bf16),
            shape((HID, 32), bf16),
            shape((2 * HID, 2 * HID), bf16),
            shape((16, 2 * HID), bf16),
            shape((2 * HID, 2 * HID), bf16),
            shape((HID, 16), bf16),
        ),
        in_specs=[SMEM] * 3 + [VMEM] * 4,
        out_specs=(VMEM,) * 8,
        compiler_params=room(2),
    )(offsets, order, cond, w_in, w_mid, w_out.T, cot_image[0])
    depth = NZ // GROUP
    slabs = [
        pltpu.VMEM((depth, 32, RAYS), bf16),
        pltpu.VMEM((depth, 2 * HID, RAYS), bf16),
        pltpu.VMEM((depth, 2 * HID, RAYS), bf16),
        *[pltpu.VMEM((depth, HID, RAYS), f32)] * 4,
        *[pltpu.VMEM((HID, RAYS), f32)] * 2,
    ]
    image, grads = pl.pallas_call(
        render_kernel,
        out_shape=(shape((3, ROWS, PY)), shape((PIECES, 1, TILES * HID))),
        in_specs=[VMEM] * 9,
        out_specs=(VMEM, VMEM),
        scratch_shapes=[
            *slabs * GROUP,
            pltpu.VMEM((ROWS, NZ * 8, PY), f32),
            pltpu.VMEM((ROWS, NZ * 8, PY), f32),
            pltpu.VMEM((2 * HID, 2 * HID), f32),
            pltpu.VMEM((2 * HID, 32), f32),
            pltpu.VMEM((16, 2 * HID), f32),
        ],
        compiler_params=pltpu.CompilerParams(
            vmem_limit_bytes=34 * 2**20
        ),
    )(slices, *prepared)

    def total(parts):
        return pl.pallas_call(
            sum_kernel,
            out_shape=shape(parts.shape),
            in_specs=[VMEM],
            out_specs=VMEM,
            compiler_params=room(2),
        )(parts)

    parts = total(exchange(grads, NEAR))
    parts = total(exchange(parts, FAR))
    packed = exchange(parts, NEAR)
    grad_in, grad_mid, grad_out_t = pl.pallas_call(
        unpack_kernel,
        out_shape=(shape((CH + COND, HID)), shape((HID, HID)), shape((4, HID))),
        in_specs=[VMEM],
        out_specs=(VMEM,) * 3,
        compiler_params=room(2),
    )(packed)
    return image[None], grad_in, grad_mid, grad_out_t.T


def solution(mesh):
    torus = Mesh(
        mesh.devices.reshape(2, 2, 8, 4, 2), ("y_far", "y_near", "z", "x", "core")
    )
    return jax.shard_map(
        per_device,
        mesh=torus,
        in_specs=(
            P(BRICK, None, None, None),
            P(VIEW, None),
            P(VIEW, None),
            P(VIEW),
            P(VIEW, None),
            P(),
            P(),
            P(),
            P(VIEW, None, BRICK, None),
        ),
        out_specs=(P(VIEW, None, BRICK, None), P(), P(), P()),
        check_vma=False,
    )
```

```python
import functools

import jax
import jax.numpy as jnp
from jax import lax
from jax.experimental import pallas as pl
from jax.experimental.pallas import tpu as pltpu
from jax.sharding import Mesh
from jax.sharding import PartitionSpec as P

VIEW = ("y_far", "y_near", "z")
BRICK = ("x", "core")
NEAR = ("y_near", "x", "core")
FAR = ("y_far", "z")

STEP_DEPTH = 0.15
NZ, CH, COND, HID = 16, 8, 8, 128
PX, PY = 32, 128
ROWS = 4
RAYS = ROWS * PY
PIECES, TILES = 16, 10
GROUP = 4

bf16, f32 = jnp.bfloat16, jnp.float32
VMEM = pl.BlockSpec(memory_space=pltpu.VMEM)
SMEM = pl.BlockSpec(memory_space=pltpu.SMEM)


def split(value):
    high = value.astype(bf16)
    return high, (value - high.astype(f32)).astype(bf16)


def split3(value):
    high = value.astype(bf16).astype(f32)
    rest = value - high
    middle = rest.astype(bf16).astype(f32)
    return high, middle, rest - middle


def mul(a, b):
    return jnp.dot(a, b, preferred_element_type=f32)


def mul_t(a, b):
    return lax.dot_general(a, b, (((1,), (1,)), ((), ())), preferred_element_type=f32)


def two_halves(value):
    return value[: value.shape[0] // 2] + value[value.shape[0] // 2 :]


def two_sides(value):
    return value[:, : value.shape[1] // 2] + value[:, value.shape[1] // 2 :]


def get(ref, rows):
    return jnp.concatenate([ref[r, rows, :] for r in range(ROWS)], 1)


def put(ref, rows, value):
    for r in range(ROWS):
        ref[r, rows, :] = value[:, r * PY : (r + 1) * PY]


def resample_kernel(offsets, shifts, volume, out):
    f_row, f_col = offsets[0, 0], offsets[0, 1]
    row_shift = shifts[0, 0] & (PX - 1)
    col_shift = shifts[0, 1] & (PY - 1)
    roll_near = (PY - col_shift) & (PY - 1)
    roll_far = (PY - 1 - col_shift) & (PY - 1)

    for s in range(2):

        def source(i):
            row = (i + row_shift) & (PX - 1)
            return volume[pl.ds(s * CH * PX + row, CH, stride=PX), :]

        near = source(0)
        for i in range(PX):
            far = source(i + 1)
            row = (1.0 - f_row) * near + f_row * far
            near = far
            value = (1.0 - f_col) * pltpu.roll(row, roll_near, 1) + f_col * pltpu.roll(
                row, roll_far, 1
            )
            out[i // ROWS, s, i % ROWS] = value


def prepare_kernel(
    offsets, order, cond, w_in, w_mid, w_out_t, cot_rows, per_ray, per_channel, masks, lhs_in, lhs_mid, lhs_out, back_mid, back_out
):
    half_in = 0.5 * w_in[...]
    high, low = split(half_in[:CH])
    high, low = high.astype(f32), low.astype(f32)
    bias = cond[0, 0] * half_in[CH : CH + 1]
    for c in range(1, COND):
        bias = bias + cond[0, c] * half_in[CH + c : CH + c + 1]
    rows = jnp.concatenate([high, high, low, *split3(bias), jnp.zeros((5, HID), f32)], 0)
    lhs_in[...] = rows.T.astype(bf16)

    half_mid = 0.5 * w_mid[...]
    high, low = split(half_mid.T)
    lhs_mid[...] = jnp.concatenate([high, high, low], 1)
    high, low = split(half_mid)
    back_mid[...] = jnp.concatenate([high, high, low], 1)

    out_t = w_out_t[...]
    high, low = split(out_t)
    high, low = high.astype(f32), low.astype(f32)
    pair = jnp.concatenate([high, low, jnp.zeros((8, HID), f32)], 0).astype(bf16)
    lhs_out[:, :HID] = pair
    lhs_out[:, HID:] = pair
    rows = 0.5 * jnp.concatenate([high, high, low, jnp.zeros((4, HID), f32)], 0)
    back_out[...] = rows.T.astype(bf16)

    for c in range(3):
        for r in range(ROWS):
            per_ray[c : c + 1, r * PY : (r + 1) * PY] = cot_rows[c, r : r + 1, :]
    per_ray[3:] = jnp.full((5, RAYS), offsets[0, 2], f32)
    for c in range(COND):
        per_channel[c : c + 1] = jnp.full((1, HID), cond[0, c], f32)

    row = lax.broadcasted_iota(jnp.int32, (2 * NZ, 3 * NZ), 0)
    column = lax.broadcasted_iota(jnp.int32, (2 * NZ, 3 * NZ), 1) & (NZ - 1)
    ahead = ((row & (NZ - 1)) - column) * (1 - 2 * order[0])
    ahead = jnp.where(row < NZ, ahead, -ahead)
    masks[...] = jnp.where(ahead > 0, 1.0, 0.0).astype(bf16)


def activate(half):
    up = 1.0 + jnp.tanh(half)
    return half * up, up


def slope_of(value, up):
    return up + value * (2.0 - up)


def softplus(x):
    z = jnp.exp(-jnp.abs(x))
    series = z * (1.0 - z * (0.5 - z * (1.0 / 3.0 - z * 0.25)))
    return jnp.maximum(x, 0.0) + jnp.where(z < 0.03, series, jnp.log(1.0 + z))


def one_minus_exp(x):
    terms = (1.0 / 2, 1.0 / 3, 1.0 / 4, 1.0 / 5, 1.0 / 6, 1.0 / 7)
    series = jnp.ones_like(x)
    for factor in reversed(terms):
        series = 1.0 - x * factor * series
    return jnp.where(x < 0.25, x * series, 1.0 - jnp.exp(-x))


def logistic(x):
    return 1.0 / (1.0 + jnp.exp(-x))


def render_kernel(
    slices,
    per_ray,
    per_channel,
    masks,
    lhs_in,
    lhs_mid,
    lhs_out,
    back_mid,
    back_out,
    image_far,
    grads,
    *scratch,
):
    raw, graw, acc_mid, acc_in, acc_out, image, sem = scratch[-7:]
    sets = [scratch[9 * p : 9 * p + 9] for p in range(GROUP)]
    feats, h1, h2, value1, up1, value2, up2, delta2, delta1 = zip(*sets)

    def layer_in(i, p):
        k = GROUP * i + p
        f_depth = per_ray[3:4, :PY]
        f_next = jnp.where(k == NZ - 1, 0.0, f_depth)
        after = jnp.minimum(k + 1, NZ - 1)
        x = jnp.concatenate(
            [(1.0 - f_depth) * slices[k, r] + f_next * slices[after, r] for r in range(ROWS)], 1
        )
        high = x.astype(bf16).astype(f32)
        features = jnp.concatenate([high, x - high, high, jnp.ones_like(x)], 0).astype(bf16)
        feats[p][i] = features
        value, up = activate(mul(lhs_in[...], features))
        value1[p][i] = value
        up1[p][i] = up
        h1[p][i, :HID], h1[p][i, HID:] = split(value)

    def layer_mid(i, p):
        value, up = activate(mul(lhs_mid[...], jnp.concatenate([h1[p][i], h1[p][i, :HID]], 0)))
        value2[p][i] = value
        up2[p][i] = up
        h2[p][i, :HID], h2[p][i, HID:] = split(value)

    def layer_out(i, p):
        result = mul(lhs_out[...], h2[p][i])[:8]
        row = pl.multiple_of(8 * GROUP * i + 8 * p, 8)
        put(raw, pl.ds(row, 8), result + pltpu.roll(result, 4, 0))

    pipeline(layer_in, layer_mid, layer_out)

    def strided(ref, o):
        return get(ref, pl.ds(o, NZ, stride=8))

    def summed(mask, value):
        return mul(mask, jnp.concatenate(split3(value), 0).astype(bf16))

    raw_sigma = strided(raw, 0)
    optical = STEP_DEPTH * softplus(raw_sigma)
    transmit = jnp.exp(-summed(masks[:NZ], optical))
    weight = transmit * one_minus_exp(optical)
    gain = jnp.zeros_like(weight)
    for c in range(3):
        rgb = logistic(strided(raw, c + 1))
        picture = jnp.sum(weight * rgb, 0, keepdims=True)
        for r in range(ROWS):
            image[c, r : r + 1, :] = picture[:, r * PY : (r + 1) * PY]
        cot_c = per_ray[c : c + 1, :]
        gain = gain + cot_c * rgb
        put(graw, pl.ds(c + 1, NZ, stride=8), weight * cot_c * (rgb * (1.0 - rgb)))
    leaving = pltpu.make_async_copy(image, image_far, sem)
    leaving.start()
    grad_optical = gain * transmit * jnp.exp(-optical) - summed(masks[NZ:], gain * weight)
    put(graw, pl.ds(0, NZ, stride=8), STEP_DEPTH * grad_optical * logistic(raw_sigma))

    acc_mid[...] = jnp.zeros_like(acc_mid)
    acc_in[...] = jnp.zeros_like(acc_in)
    acc_out[...] = jnp.zeros_like(acc_out)
    first = lax.broadcasted_iota(jnp.int32, (8, RAYS), 0) < 4

    def back_from_out(i, p):
        g = get(graw, pl.ds(pl.multiple_of(8 * GROUP * i + 8 * p, 8), 8))
        g = jnp.where(first, g, pltpu.roll(g, 4, 0))
        high = g.astype(bf16).astype(f32)
        pair = jnp.where(first, high, g - high)
        cotangent = jnp.concatenate([pair, jnp.where(first, high, 0.0)], 0).astype(bf16)
        delta2[p][...] = mul(back_out[...], cotangent) * slope_of(value2[p][i], up2[p][i])
        acc_out[...] += mul_t(cotangent, h2[p][i])

    def back_from_mid(i, p):
        pair = jnp.concatenate(split(delta2[p][...]), 0)
        acc_mid[...] += mul_t(h1[p][i], pair)
        delta1[p][...] = mul(back_mid[...], jnp.concatenate([pair, pair[:HID]], 0)) * slope_of(value1[p][i], up1[p][i])

    def back_from_in(i, p):
        pair = jnp.concatenate(split(delta1[p][...]), 0)
        acc_in[...] += mul_t(pair, feats[p][i])

    pipeline(back_from_out, back_from_mid, back_from_in)

    total = two_halves(acc_in[...]).T
    rows_in = total[:CH] + total[CH : 2 * CH]
    rows_cond = per_channel[...] * total[3 * CH : 3 * CH + 1]
    total = two_sides(acc_out[...])[:8]
    rows_out = total + pltpu.roll(total, 4, 0)
    packed = jnp.concatenate(
        [
            two_sides(two_halves(acc_mid[...])),
            rows_in,
            rows_cond,
            rows_out,
            jnp.zeros((8, HID), f32),
        ],
        0,
    )
    for t in range(TILES):
        grads[:, 0, t * HID : (t + 1) * HID] = packed[t * PIECES : (t + 1) * PIECES]
    leaving.wait()


def pipeline(first, second, third):
    def step(i, carry):
        for p in group:
            third(i - 2, p)
        for p in group:
            second(i - 1, p)
        for p in group:
            first(i, p)
        return carry

    group = range(GROUP)
    last = NZ // GROUP - 1
    [first(0, p) for p in group]
    [second(0, p) for p in group]
    [first(1, p) for p in group]
    lax.fori_loop(2, last + 1, step, 0)
    [third(last - 1, p) for p in group]
    [second(last, p) for p in group]
    [third(last, p) for p in group]


def sum_kernel(parts, out):
    total = parts[0]
    for i in range(1, PIECES):
        total = total + parts[i]
    for i in range(PIECES):
        out[i] = total


def unpack_kernel(packed, grad_in, grad_mid, grad_out_t):
    def rows(t):
        return packed[:, 0, t * HID : (t + 1) * HID]

    for t in range(HID // PIECES):
        grad_mid[t * PIECES : (t + 1) * PIECES] = rows(t)
    grad_in[...] = rows(HID // PIECES)
    grad_out_t[...] = rows(HID // PIECES + 1)[:4]


def room(mebibytes):
    return pltpu.CompilerParams(vmem_limit_bytes=mebibytes * 2**20)


def shape(dims, dtype=f32):
    return jax.ShapeDtypeStruct(dims, dtype)


def exchange(parts, axes):
    return lax.all_to_all(parts, axes, 0, 0, tiled=True)


def per_device(volume, offsets, shifts, order, cond, w_in, w_mid, w_out, cot_image):
    rows = pl.pallas_call(
        resample_kernel,
        out_shape=shape((8, 2, ROWS, CH, PY)),
        in_specs=[SMEM, SMEM, VMEM],
        out_specs=VMEM,
    )(offsets, shifts, volume.reshape(2 * CH * PX, PY))
    slices = exchange(rows, BRICK).reshape(NZ, ROWS, CH, PY)
    prepared = pl.pallas_call(
        prepare_kernel,
        out_shape=(
            shape((8, RAYS)),
            shape((COND, HID)),
            shape((2 * NZ, 3 * NZ), bf16),
            shape((HID, 32), bf16),
            shape((HID, 3 * HID), bf16),
            shape((16, 2 * HID), bf16),
            shape((HID, 3 * HID), bf16),
            shape((HID, 16), bf16),
        ),
        in_specs=[SMEM] * 3 + [VMEM] * 4,
        out_specs=(VMEM,) * 8,
        compiler_params=room(2),
    )(offsets, order, cond, w_in, w_mid, w_out.T, cot_image[0])
    depth = NZ // GROUP
    slabs = [
        pltpu.VMEM((depth, 32, RAYS), bf16),
        pltpu.VMEM((depth, 2 * HID, RAYS), bf16),
        pltpu.VMEM((depth, 2 * HID, RAYS), bf16),
        *[pltpu.VMEM((depth, HID, RAYS), f32)] * 4,
        *[pltpu.VMEM((HID, RAYS), f32)] * 2,
    ]
    image, grads = pl.pallas_call(
        render_kernel,
        out_shape=(shape((3, ROWS, PY)), shape((PIECES, 1, TILES * HID))),
        in_specs=[VMEM] * 9,
        out_specs=(pl.BlockSpec(memory_space=pl.ANY), VMEM),
        scratch_shapes=[
            *slabs * GROUP,
            pltpu.VMEM((ROWS, NZ * 8, PY), f32),
            pltpu.VMEM((ROWS, NZ * 8, PY), f32),
            pltpu.VMEM((2 * HID, 2 * HID), f32),
            pltpu.VMEM((2 * HID, 32), f32),
            pltpu.VMEM((16, 2 * HID), f32),
            pltpu.VMEM((3, ROWS, PY), f32),
            pltpu.SemaphoreType.DMA,
        ],
        compiler_params=pltpu.CompilerParams(
            vmem_limit_bytes=34 * 2**20
        ),
    )(slices, *prepared)

    def total(parts):
        return pl.pallas_call(
            sum_kernel,
            out_shape=shape(parts.shape),
            in_specs=[VMEM],
            out_specs=VMEM,
            compiler_params=room(2),
        )(parts)

    parts = total(exchange(grads, NEAR))
    parts = total(exchange(parts, FAR))
    packed = exchange(parts, NEAR)
    grad_in, grad_mid, grad_out_t = pl.pallas_call(
        unpack_kernel,
        out_shape=(shape((CH + COND, HID)), shape((HID, HID)), shape((4, HID))),
        in_specs=[VMEM],
        out_specs=(VMEM,) * 3,
        compiler_params=room(2),
    )(packed)
    return image[None], grad_in, grad_mid, grad_out_t.T


def solution(mesh):
    torus = Mesh(
        mesh.devices.reshape(2, 2, 8, 4, 2), ("y_far", "y_near", "z", "x", "core")
    )
    return jax.shard_map(
        per_device,
        mesh=torus,
        in_specs=(
            P(BRICK, None, None, None),
            P(VIEW, None),
            P(VIEW, None),
            P(VIEW),
            P(VIEW, None),
            P(),
            P(),
            P(),
            P(VIEW, None, BRICK, None),
        ),
        out_specs=(P(VIEW, None, BRICK, None), P(), P(), P()),
        check_vma=False,
    )
```

```python
import functools

import jax
import jax.numpy as jnp
from jax import lax
from jax.experimental import pallas as pl
from jax.experimental.pallas import tpu as pltpu
from jax.sharding import Mesh
from jax.sharding import PartitionSpec as P

VIEW = ("y_far", "y_near", "z")
BRICK = ("x", "core")
NEAR = ("y_near", "x", "core")
FAR = ("y_far", "z")

STEP_DEPTH = 0.15
NZ, CH, COND, HID = 16, 8, 8, 128
PX, PY = 32, 128
ROWS = 4
RAYS = ROWS * PY
HALVES = slice(0, RAYS // 2), slice(RAYS // 2, RAYS)
PIECES, TILES = 16, 10
GROUP = 4

bf16, f32 = jnp.bfloat16, jnp.float32
VMEM = pl.BlockSpec(memory_space=pltpu.VMEM)
SMEM = pl.BlockSpec(memory_space=pltpu.SMEM)


def split(value):
    high = value.astype(bf16)
    return high, (value - high.astype(f32)).astype(bf16)


def split3(value):
    high = value.astype(bf16).astype(f32)
    rest = value - high
    middle = rest.astype(bf16).astype(f32)
    return high, middle, rest - middle


def mul(a, b):
    return jnp.dot(a, b, preferred_element_type=f32)


def mul_t(a, b):
    return lax.dot_general(a, b, (((1,), (1,)), ((), ())), preferred_element_type=f32)


def two_halves(value):
    return value[: value.shape[0] // 2] + value[value.shape[0] // 2 :]


def two_sides(value):
    return value[:, : value.shape[1] // 2] + value[:, value.shape[1] // 2 :]


def get(ref, rows):
    return jnp.concatenate([ref[r, rows, :] for r in range(ROWS)], 1)


def put(ref, rows, value):
    for r in range(ROWS):
        ref[r, rows, :] = value[:, r * PY : (r + 1) * PY]


def resample_kernel(offsets, shifts, volume, out):
    f_row, f_col = offsets[0, 0], offsets[0, 1]
    row_shift = shifts[0, 0] & (PX - 1)
    col_shift = shifts[0, 1] & (PY - 1)
    roll_near = (PY - col_shift) & (PY - 1)
    roll_far = (PY - 1 - col_shift) & (PY - 1)

    for s in range(2):

        def source(i):
            row = (i + row_shift) & (PX - 1)
            return volume[pl.ds(s * CH * PX + row, CH, stride=PX), :]

        near = source(0)
        for i in range(PX):
            far = source(i + 1)
            row = (1.0 - f_row) * near + f_row * far
            near = far
            value = (1.0 - f_col) * pltpu.roll(row, roll_near, 1) + f_col * pltpu.roll(
                row, roll_far, 1
            )
            out[i // ROWS, s, i % ROWS] = value


def prepare_kernel(
    offsets, order, cond, w_in, w_mid, w_out_t, cot_rows, per_ray, per_channel, masks, lhs_in, lhs_mid, lhs_out, back_mid, back_out
):
    half_in = 0.5 * w_in[...]
    high, low = split(half_in[:CH])
    high, low = high.astype(f32), low.astype(f32)
    bias = cond[0, 0] * half_in[CH : CH + 1]
    for c in range(1, COND):
        bias = bias + cond[0, c] * half_in[CH + c : CH + c + 1]
    rows = jnp.concatenate([high, high, low, *split3(bias), jnp.zeros((5, HID), f32)], 0)
    lhs_in[...] = rows.T.astype(bf16)

    half_mid = 0.5 * w_mid[...]
    high, low = split(half_mid.T)
    lhs_mid[:HID, :HID] = high
    lhs_mid[:HID, HID:] = high
    lhs_mid[HID:, :HID] = low
    lhs_mid[HID:, HID:] = low
    high, low = split(half_mid)
    back_mid[:HID, :HID] = high
    back_mid[:HID, HID:] = high
    back_mid[HID:, :HID] = low
    back_mid[HID:, HID:] = low

    out_t = w_out_t[...]
    high, low = split(out_t)
    high, low = high.astype(f32), low.astype(f32)
    pair = jnp.concatenate([high, low, jnp.zeros((8, HID), f32)], 0).astype(bf16)
    lhs_out[:, :HID] = pair
    lhs_out[:, HID:] = pair
    rows = 0.5 * jnp.concatenate([high, high, low, jnp.zeros((4, HID), f32)], 0)
    back_out[...] = rows.T.astype(bf16)

    for c in range(3):
        for r in range(ROWS):
            per_ray[c : c + 1, r * PY : (r + 1) * PY] = cot_rows[c, r : r + 1, :]
    per_ray[3:] = jnp.full((5, RAYS), offsets[0, 2], f32)
    for c in range(COND):
        per_channel[c : c + 1] = jnp.full((1, HID), cond[0, c], f32)

    row = lax.broadcasted_iota(jnp.int32, (2 * NZ, 3 * NZ), 0)
    column = lax.broadcasted_iota(jnp.int32, (2 * NZ, 3 * NZ), 1) & (NZ - 1)
    ahead = ((row & (NZ - 1)) - column) * (1 - 2 * order[0])
    ahead = jnp.where(row < NZ, ahead, -ahead)
    masks[...] = jnp.where(ahead > 0, 1.0, 0.0).astype(bf16)


def activate(half):
    up = 1.0 + jnp.tanh(half)
    return half * up, up


def slope_of(value, up):
    return up + value * (2.0 - up)


def softplus(x):
    z = jnp.exp(-jnp.abs(x))
    series = z * (1.0 - z * (0.5 - z * (1.0 / 3.0 - z * 0.25)))
    return jnp.maximum(x, 0.0) + jnp.where(z < 0.03, series, jnp.log(1.0 + z))


def one_minus_exp(x):
    terms = (1.0 / 2, 1.0 / 3, 1.0 / 4, 1.0 / 5, 1.0 / 6, 1.0 / 7)
    series = jnp.ones_like(x)
    for factor in reversed(terms):
        series = 1.0 - x * factor * series
    return jnp.where(x < 0.25, x * series, 1.0 - jnp.exp(-x))


def logistic(x):
    return 1.0 / (1.0 + jnp.exp(-x))


def render_kernel(
    slices,
    per_ray,
    per_channel,
    masks,
    lhs_in,
    lhs_mid,
    lhs_out,
    back_mid,
    back_out,
    image,
    grads,
    *scratch,
):
    raw, graw, acc_mid, acc_in, acc_out = scratch[-5:]
    sets = [scratch[9 * p : 9 * p + 9] for p in range(GROUP)]
    feats, h1, h2, value1, up1, value2, up2, delta2, delta1 = zip(*sets)

    def layer_in(i, p):
        k = GROUP * i + p
        f_depth = per_ray[3:4, :PY]
        f_next = jnp.where(k == NZ - 1, 0.0, f_depth)
        after = jnp.minimum(k + 1, NZ - 1)
        x = jnp.concatenate(
            [(1.0 - f_depth) * slices[k, r] + f_next * slices[after, r] for r in range(ROWS)], 1
        )
        high = x.astype(bf16).astype(f32)
        features = jnp.concatenate([high, x - high, high, jnp.ones_like(x)], 0).astype(bf16)
        feats[p][i] = features
        for half in HALVES:
            value, up = activate(mul(lhs_in[...], features[:, half]))
            value1[p][i, :, half] = value
            up1[p][i, :, half] = up
            h1[p][i, :HID, half], h1[p][i, HID:, half] = split(value)

    def layer_mid(i, p):
        for half in HALVES:
            value, up = activate(two_halves(mul(lhs_mid[...], h1[p][i, :, half])))
            value2[p][i, :, half] = value
            up2[p][i, :, half] = up
            h2[p][i, :HID, half], h2[p][i, HID:, half] = split(value)

    def layer_out(i, p):
        result = mul(lhs_out[...], h2[p][i])[:8]
        row = pl.multiple_of(8 * GROUP * i + 8 * p, 8)
        put(raw, pl.ds(row, 8), result + pltpu.roll(result, 4, 0))

    pipeline(layer_in, layer_mid, layer_out)

    def strided(ref, o):
        return get(ref, pl.ds(o, NZ, stride=8))

    def summed(mask, value):
        return mul(mask, jnp.concatenate(split3(value), 0).astype(bf16))

    raw_sigma = strided(raw, 0)
    optical = STEP_DEPTH * softplus(raw_sigma)
    transmit = jnp.exp(-summed(masks[:NZ], optical))
    weight = transmit * one_minus_exp(optical)
    gain = jnp.zeros_like(weight)
    for c in range(3):
        rgb = logistic(strided(raw, c + 1))
        picture = jnp.sum(weight * rgb, 0, keepdims=True)
        for r in range(ROWS):
            image[c, r : r + 1, :] = picture[:, r * PY : (r + 1) * PY]
        cot_c = per_ray[c : c + 1, :]
        gain = gain + cot_c * rgb
        put(graw, pl.ds(c + 1, NZ, stride=8), weight * cot_c * (rgb * (1.0 - rgb)))
    grad_optical = gain * transmit * jnp.exp(-optical) - summed(masks[NZ:], gain * weight)
    put(graw, pl.ds(0, NZ, stride=8), STEP_DEPTH * grad_optical * logistic(raw_sigma))

    acc_mid[...] = jnp.zeros_like(acc_mid)
    acc_in[...] = jnp.zeros_like(acc_in)
    acc_out[...] = jnp.zeros_like(acc_out)
    first = lax.broadcasted_iota(jnp.int32, (8, RAYS), 0) < 4

    def back_from_out(i, p):
        g = get(graw, pl.ds(pl.multiple_of(8 * GROUP * i + 8 * p, 8), 8))
        g = jnp.where(first, g, pltpu.roll(g, 4, 0))
        high = g.astype(bf16).astype(f32)
        pair = jnp.where(first, high, g - high)
        cotangent = jnp.concatenate([pair, jnp.where(first, high, 0.0)], 0).astype(bf16)
        for half in HALVES:
            slope = slope_of(value2[p][i, :, half], up2[p][i, :, half])
            delta2[p][:, half] = mul(back_out[...], cotangent[:, half]) * slope
        acc_out[...] += mul_t(cotangent, h2[p][i])

    def back_from_mid(i, p):
        pair = jnp.concatenate(split(delta2[p][...]), 0)
        acc_mid[...] += mul_t(h1[p][i], pair)
        for half in HALVES:
            slope = slope_of(value1[p][i, :, half], up1[p][i, :, half])
            delta1[p][:, half] = two_halves(mul(back_mid[...], pair[:, half])) * slope

    def back_from_in(i, p):
        pair = jnp.concatenate(split(delta1[p][...]), 0)
        acc_in[...] += mul_t(pair, feats[p][i])

    pipeline(back_from_out, back_from_mid, back_from_in)

    total = two_halves(acc_in[...]).T
    rows_in = total[:CH] + total[CH : 2 * CH]
    rows_cond = per_channel[...] * total[3 * CH : 3 * CH + 1]
    total = two_sides(acc_out[...])[:8]
    rows_out = total + pltpu.roll(total, 4, 0)
    packed = jnp.concatenate(
        [
            two_sides(two_halves(acc_mid[...])),
            rows_in,
            rows_cond,
            rows_out,
            jnp.zeros((8, HID), f32),
        ],
        0,
    )
    for t in range(TILES):
        grads[:, 0, t * HID : (t + 1) * HID] = packed[t * PIECES : (t + 1) * PIECES]


def pipeline(first, second, third):
    def step(i, carry):
        for p in group:
            third(i - 2, p)
        for p in group:
            second(i - 1, p)
        for p in group:
            first(i, p)
        return carry

    group = range(GROUP)
    last = NZ // GROUP - 1
    [first(0, p) for p in group]
    [second(0, p) for p in group]
    [first(1, p) for p in group]
    lax.fori_loop(2, last + 1, step, 0)
    [third(last - 1, p) for p in group]
    [second(last, p) for p in group]
    [third(last, p) for p in group]


def sum_kernel(parts, out):
    total = parts[0]
    for i in range(1, PIECES):
        total = total + parts[i]
    for i in range(PIECES):
        out[i] = total


def unpack_kernel(packed, grad_in, grad_mid, grad_out_t):
    def rows(t):
        return packed[:, 0, t * HID : (t + 1) * HID]

    for t in range(HID // PIECES):
        grad_mid[t * PIECES : (t + 1) * PIECES] = rows(t)
    grad_in[...] = rows(HID // PIECES)
    grad_out_t[...] = rows(HID // PIECES + 1)[:4]


def room(mebibytes):
    return pltpu.CompilerParams(vmem_limit_bytes=mebibytes * 2**20)


def shape(dims, dtype=f32):
    return jax.ShapeDtypeStruct(dims, dtype)


def exchange(parts, axes):
    return lax.all_to_all(parts, axes, 0, 0, tiled=True)


def per_device(volume, offsets, shifts, order, cond, w_in, w_mid, w_out, cot_image):
    rows = pl.pallas_call(
        resample_kernel,
        out_shape=shape((8, 2, ROWS, CH, PY)),
        in_specs=[SMEM, SMEM, VMEM],
        out_specs=VMEM,
    )(offsets, shifts, volume.reshape(2 * CH * PX, PY))
    slices = exchange(rows, BRICK).reshape(NZ, ROWS, CH, PY)
    prepared = pl.pallas_call(
        prepare_kernel,
        out_shape=(
            shape((8, RAYS)),
            shape((COND, HID)),
            shape((2 * NZ, 3 * NZ), bf16),
            shape((HID, 32), bf16),
            shape((2 * HID, 2 * HID), bf16),
            shape((16, 2 * HID), bf16),
            shape((2 * HID, 2 * HID), bf16),
            shape((HID, 16), bf16),
        ),
        in_specs=[SMEM] * 3 + [VMEM] * 4,
        out_specs=(VMEM,) * 8,
        compiler_params=room(2),
    )(offsets, order, cond, w_in, w_mid, w_out.T, cot_image[0])
    depth = NZ // GROUP
    slabs = [
        pltpu.VMEM((depth, 32, RAYS), bf16),
        pltpu.VMEM((depth, 2 * HID, RAYS), bf16),
        pltpu.VMEM((depth, 2 * HID, RAYS), bf16),
        *[pltpu.VMEM((depth, HID, RAYS), f32)] * 4,
        *[pltpu.VMEM((HID, RAYS), f32)] * 2,
    ]
    image, grads = pl.pallas_call(
        render_kernel,
        out_shape=(shape((3, ROWS, PY)), shape((PIECES, 1, TILES * HID))),
        in_specs=[VMEM] * 9,
        out_specs=(VMEM, VMEM),
        scratch_shapes=[
            *slabs * GROUP,
            pltpu.VMEM((ROWS, NZ * 8, PY), f32),
            pltpu.VMEM((ROWS, NZ * 8, PY), f32),
            pltpu.VMEM((2 * HID, 2 * HID), f32),
            pltpu.VMEM((2 * HID, 32), f32),
            pltpu.VMEM((16, 2 * HID), f32),
        ],
        compiler_params=pltpu.CompilerParams(
            vmem_limit_bytes=34 * 2**20
        ),
    )(slices, *prepared)

    def total(parts):
        return pl.pallas_call(
            sum_kernel,
            out_shape=shape(parts.shape),
            in_specs=[VMEM],
            out_specs=VMEM,
            compiler_params=room(2),
        )(parts)

    parts = total(exchange(grads, NEAR))
    parts = total(exchange(parts, FAR))
    packed = exchange(parts, NEAR)
    grad_in, grad_mid, grad_out_t = pl.pallas_call(
        unpack_kernel,
        out_shape=(shape((CH + COND, HID)), shape((HID, HID)), shape((4, HID))),
        in_specs=[VMEM],
        out_specs=(VMEM,) * 3,
        compiler_params=room(2),
    )(packed)
    return image[None], grad_in, grad_mid, grad_out_t.T


def solution(mesh):
    torus = Mesh(
        mesh.devices.reshape(2, 2, 8, 4, 2), ("y_far", "y_near", "z", "x", "core")
    )
    return jax.shard_map(
        per_device,
        mesh=torus,
        in_specs=(
            P(BRICK, None, None, None),
            P(VIEW, None),
            P(VIEW, None),
            P(VIEW),
            P(VIEW, None),
            P(),
            P(),
            P(),
            P(VIEW, None, BRICK, None),
        ),
        out_specs=(P(VIEW, None, BRICK, None), P(), P(), P()),
        check_vma=False,
    )
```

```python
import functools

import jax
import jax.numpy as jnp
from jax import lax
from jax.experimental import pallas as pl
from jax.experimental.pallas import tpu as pltpu
from jax.sharding import Mesh
from jax.sharding import PartitionSpec as P

VIEW = ("y_far", "y_near", "z")
BRICK = ("x", "core")
NEAR = ("y_near", "x", "core")
FAR = ("y_far", "z")

STEP_DEPTH = 0.15
NZ, CH, COND, HID = 16, 8, 8, 128
PX, PY = 32, 128
ROWS = 4
RAYS = ROWS * PY
PIECES, TILES = 16, 10
GROUP = 4

bf16, f32 = jnp.bfloat16, jnp.float32
VMEM = pl.BlockSpec(memory_space=pltpu.VMEM)
SMEM = pl.BlockSpec(memory_space=pltpu.SMEM)


def split(value):
    high = value.astype(bf16)
    return high, (value - high.astype(f32)).astype(bf16)


def split3(value):
    high = value.astype(bf16).astype(f32)
    rest = value - high
    middle = rest.astype(bf16).astype(f32)
    return high, middle, rest - middle


def mul(a, b):
    return jnp.dot(a, b, preferred_element_type=f32)


def mul_t(a, b):
    return lax.dot_general(a, b, (((1,), (1,)), ((), ())), preferred_element_type=f32)


def two_halves(value):
    return value[: value.shape[0] // 2] + value[value.shape[0] // 2 :]


def two_sides(value):
    return value[:, : value.shape[1] // 2] + value[:, value.shape[1] // 2 :]


def get(ref, rows):
    return jnp.concatenate([ref[r, rows, :] for r in range(ROWS)], 1)


def put(ref, rows, value):
    for r in range(ROWS):
        ref[r, rows, :] = value[:, r * PY : (r + 1) * PY]


def resample_kernel(offsets, shifts, volume, out):
    f_row, f_col = offsets[0, 0], offsets[0, 1]
    row_shift = shifts[0, 0] & (PX - 1)
    col_shift = shifts[0, 1] & (PY - 1)
    roll_near = (PY - col_shift) & (PY - 1)
    roll_far = (PY - 1 - col_shift) & (PY - 1)

    for s in range(2):

        def source(i):
            row = (i + row_shift) & (PX - 1)
            return volume[pl.ds(s * CH * PX + row, CH, stride=PX), :]

        near = source(0)
        for i in range(PX):
            far = source(i + 1)
            row = (1.0 - f_row) * near + f_row * far
            near = far
            value = (1.0 - f_col) * pltpu.roll(row, roll_near, 1) + f_col * pltpu.roll(
                row, roll_far, 1
            )
            out[i // ROWS, s, i % ROWS] = value


def prepare_kernel(
    offsets, order, cond, w_in, w_mid, w_out_t, cot_rows, per_ray, per_channel, masks, lhs_in, lhs_mid, lhs_out, back_mid, back_out
):
    half_in = 0.5 * w_in[...]
    high, low = split(half_in[:CH])
    high, low = high.astype(f32), low.astype(f32)
    bias = cond[0, 0] * half_in[CH : CH + 1]
    for c in range(1, COND):
        bias = bias + cond[0, c] * half_in[CH + c : CH + c + 1]
    rows = jnp.concatenate([high, high, low, *split3(bias), jnp.zeros((5, HID), f32)], 0)
    lhs_in[...] = rows.T.astype(bf16)

    half_mid = 0.5 * w_mid[...]
    high, low = split(half_mid.T)
    lhs_mid[:HID, :HID] = high
    lhs_mid[:HID, HID:] = high
    lhs_mid[HID:, :HID] = low
    lhs_mid[HID:, HID:] = low
    high, low = split(half_mid)
    back_mid[:HID, :HID] = high
    back_mid[:HID, HID:] = high
    back_mid[HID:, :HID] = low
    back_mid[HID:, HID:] = low

    out_t = w_out_t[...]
    high, low = split(out_t)
    high, low = high.astype(f32), low.astype(f32)
    pair = jnp.concatenate([high, low, jnp.zeros((8, HID), f32)], 0).astype(bf16)
    lhs_out[:, :HID] = pair
    lhs_out[:, HID:] = pair
    rows = 0.5 * jnp.concatenate([high, high, low, jnp.zeros((4, HID), f32)], 0)
    back_out[...] = rows.T.astype(bf16)

    for c in range(3):
        for r in range(ROWS):
            per_ray[c : c + 1, r * PY : (r + 1) * PY] = cot_rows[c, r : r + 1, :]
    per_ray[3:] = jnp.full((5, RAYS), offsets[0, 2], f32)
    for c in range(COND):
        per_channel[c : c + 1] = jnp.full((1, HID), cond[0, c], f32)

    row = lax.broadcasted_iota(jnp.int32, (2 * NZ, 3 * NZ), 0)
    column = lax.broadcasted_iota(jnp.int32, (2 * NZ, 3 * NZ), 1) & (NZ - 1)
    ahead = ((row & (NZ - 1)) - column) * (1 - 2 * order[0])
    ahead = jnp.where(row < NZ, ahead, -ahead)
    masks[...] = jnp.where(ahead > 0, 1.0, 0.0).astype(bf16)


def activate(half):
    up = 1.0 + jnp.tanh(half)
    return half * up, up


def slope_of(value, up):
    return up + value * (2.0 - up)


def softplus(x):
    z = jnp.exp(-jnp.abs(x))
    series = z * (1.0 - z * (0.5 - z * (1.0 / 3.0 - z * 0.25)))
    return jnp.maximum(x, 0.0) + jnp.where(z < 0.03, series, jnp.log(1.0 + z))


def one_minus_exp(x):
    terms = (1.0 / 2, 1.0 / 3, 1.0 / 4, 1.0 / 5, 1.0 / 6, 1.0 / 7)
    series = jnp.ones_like(x)
    for factor in reversed(terms):
        series = 1.0 - x * factor * series
    return jnp.where(x < 0.25, x * series, 1.0 - jnp.exp(-x))


def logistic(x):
    return 1.0 / (1.0 + jnp.exp(-x))


def render_kernel(
    slices,
    per_ray,
    per_channel,
    masks,
    lhs_in,
    lhs_mid,
    lhs_out,
    back_mid,
    back_out,
    image,
    grads,
    *scratch,
):
    raw, graw, acc_mid, acc_in, acc_out = scratch[-5:]
    sets = [scratch[9 * p : 9 * p + 9] for p in range(GROUP)]
    feats, h1, h2, value1, up1, value2, up2, delta2, delta1 = zip(*sets)

    def layer_in(i, p):
        k = GROUP * i + p
        f_depth = per_ray[3:4, :PY]
        f_next = jnp.where(k == NZ - 1, 0.0, f_depth)
        after = jnp.minimum(k + 1, NZ - 1)
        x = jnp.concatenate(
            [(1.0 - f_depth) * slices[k, r] + f_next * slices[after, r] for r in range(ROWS)], 1
        )
        high = x.astype(bf16).astype(f32)
        features = jnp.concatenate([high, x - high, high, jnp.ones_like(x)], 0).astype(bf16)
        feats[p][i] = features
        value, up = activate(mul(lhs_in[...], features))
        value1[p][i] = value
        up1[p][i] = up
        h1[p][i, :HID], h1[p][i, HID:] = split(value)

    def layer_mid(i, p):
        value, up = activate(two_halves(mul(lhs_mid[...], h1[p][i])))
        value2[p][i] = value
        up2[p][i] = up
        h2[p][i, :HID], h2[p][i, HID:] = split(value)

    def layer_out(i, p):
        result = mul(lhs_out[...], h2[p][i])[:8]
        row = pl.multiple_of(8 * GROUP * i + 8 * p, 8)
        put(raw, pl.ds(row, 8), result + pltpu.roll(result, 4, 0))

    pipeline(layer_in, layer_mid, layer_out)

    def strided(ref, o):
        return get(ref, pl.ds(o, NZ, stride=8))

    def summed(mask, value):
        return mul(mask, jnp.concatenate(split3(value), 0).astype(bf16))

    raw_sigma = strided(raw, 0)
    optical = STEP_DEPTH * softplus(raw_sigma)
    transmit = jnp.exp(-summed(masks[:NZ], optical))
    weight = transmit * one_minus_exp(optical)
    gain = jnp.zeros_like(weight)
    for c in range(3):
        rgb = logistic(strided(raw, c + 1))
        picture = jnp.sum(weight * rgb, 0, keepdims=True)
        for r in range(ROWS):
            image[c, r : r + 1, :] = picture[:, r * PY : (r + 1) * PY]
        cot_c = per_ray[c : c + 1, :]
        gain = gain + cot_c * rgb
        put(graw, pl.ds(c + 1, NZ, stride=8), weight * cot_c * (rgb * (1.0 - rgb)))
    grad_optical = gain * transmit * jnp.exp(-optical) - summed(masks[NZ:], gain * weight)
    put(graw, pl.ds(0, NZ, stride=8), STEP_DEPTH * grad_optical * logistic(raw_sigma))

    acc_mid[...] = jnp.zeros_like(acc_mid)
    acc_in[...] = jnp.zeros_like(acc_in)
    acc_out[...] = jnp.zeros_like(acc_out)
    first = lax.broadcasted_iota(jnp.int32, (8, RAYS), 0) < 4

    def back_from_out(i, p):
        g = get(graw, pl.ds(pl.multiple_of(8 * GROUP * i + 8 * p, 8), 8))
        g = jnp.where(first, g, pltpu.roll(g, 4, 0))
        high = g.astype(bf16).astype(f32)
        pair = jnp.where(first, high, g - high)
        cotangent = jnp.concatenate([pair, jnp.where(first, high, 0.0)], 0).astype(bf16)
        delta2[p][...] = mul(back_out[...], cotangent) * slope_of(value2[p][i], up2[p][i])
        acc_out[...] += mul_t(cotangent, h2[p][i])

    def back_from_mid(i, p):
        pair = jnp.concatenate(split(delta2[p][...]), 0)
        acc_mid[...] += mul_t(h1[p][i], pair)
        delta1[p][...] = two_halves(mul(back_mid[...], pair)) * slope_of(value1[p][i], up1[p][i])

    def back_from_in(i, p):
        pair = jnp.concatenate(split(delta1[p][...]), 0)
        acc_in[...] += mul_t(pair, feats[p][i])

    pipeline(back_from_out, back_from_mid, back_from_in)

    total = two_halves(acc_in[...]).T
    rows_in = total[:CH] + total[CH : 2 * CH]
    rows_cond = per_channel[...] * total[3 * CH : 3 * CH + 1]
    total = two_sides(acc_out[...])[:8]
    rows_out = total + pltpu.roll(total, 4, 0)
    packed = jnp.concatenate(
        [
            two_sides(two_halves(acc_mid[...])),
            rows_in,
            rows_cond,
            rows_out,
            jnp.zeros((8, HID), f32),
        ],
        0,
    )
    for t in range(TILES):
        grads[:, 0, t * HID : (t + 1) * HID] = packed[t * PIECES : (t + 1) * PIECES]


def pipeline(first, second, third):
    def step(i, carry):
        for p in group:
            third(i - 2, p)
        for p in group:
            second(i - 1, p)
        for p in group:
            first(i, p)
        return carry

    group = range(GROUP)
    last = NZ // GROUP - 1
    [first(0, p) for p in group]
    [second(0, p) for p in group]
    [first(1, p) for p in group]
    lax.fori_loop(2, last + 1, step, 0)
    [third(last - 1, p) for p in group]
    [second(last, p) for p in group]
    [third(last, p) for p in group]


def sum_kernel(parts, out):
    total = parts[0]
    for i in range(1, PIECES):
        total = total + parts[i]
    for i in range(PIECES):
        out[i] = total


def unpack_kernel(packed, grad_in, grad_mid, grad_out_t, near_in, near_mid, near_out, sems):
    def rows(t):
        return packed[:, 0, t * HID : (t + 1) * HID]

    near_in[...] = rows(HID // PIECES)
    near_out[...] = rows(HID // PIECES + 1)[:4]
    copies = [
        pltpu.make_async_copy(near_in, grad_in, sems.at[0]),
        pltpu.make_async_copy(near_out, grad_out_t, sems.at[1]),
    ]
    for t in range(HID // PIECES):
        near_mid[t * PIECES : (t + 1) * PIECES] = rows(t)
    copies.append(pltpu.make_async_copy(near_mid, grad_mid, sems.at[2]))
    for copy in copies:
        copy.start()
    for copy in copies:
        copy.wait()


def room(mebibytes):
    return pltpu.CompilerParams(vmem_limit_bytes=mebibytes * 2**20)


def shape(dims, dtype=f32):
    return jax.ShapeDtypeStruct(dims, dtype)


def exchange(parts, axes):
    return lax.all_to_all(parts, axes, 0, 0, tiled=True)


def per_device(volume, offsets, shifts, order, cond, w_in, w_mid, w_out, cot_image):
    rows = pl.pallas_call(
        resample_kernel,
        out_shape=shape((8, 2, ROWS, CH, PY)),
        in_specs=[SMEM, SMEM, VMEM],
        out_specs=VMEM,
    )(offsets, shifts, volume.reshape(2 * CH * PX, PY))
    slices = exchange(rows, BRICK).reshape(NZ, ROWS, CH, PY)
    prepared = pl.pallas_call(
        prepare_kernel,
        out_shape=(
            shape((8, RAYS)),
            shape((COND, HID)),
            shape((2 * NZ, 3 * NZ), bf16),
            shape((HID, 32), bf16),
            shape((2 * HID, 2 * HID), bf16),
            shape((16, 2 * HID), bf16),
            shape((2 * HID, 2 * HID), bf16),
            shape((HID, 16), bf16),
        ),
        in_specs=[SMEM] * 3 + [VMEM] * 4,
        out_specs=(VMEM,) * 8,
        compiler_params=room(2),
    )(offsets, order, cond, w_in, w_mid, w_out.T, cot_image[0])
    depth = NZ // GROUP
    slabs = [
        pltpu.VMEM((depth, 32, RAYS), bf16),
        pltpu.VMEM((depth, 2 * HID, RAYS), bf16),
        pltpu.VMEM((depth, 2 * HID, RAYS), bf16),
        *[pltpu.VMEM((depth, HID, RAYS), f32)] * 4,
        *[pltpu.VMEM((HID, RAYS), f32)] * 2,
    ]
    image, grads = pl.pallas_call(
        render_kernel,
        out_shape=(shape((3, ROWS, PY)), shape((PIECES, 1, TILES * HID))),
        in_specs=[VMEM] * 9,
        out_specs=(VMEM, VMEM),
        scratch_shapes=[
            *slabs * GROUP,
            pltpu.VMEM((ROWS, NZ * 8, PY), f32),
            pltpu.VMEM((ROWS, NZ * 8, PY), f32),
            pltpu.VMEM((2 * HID, 2 * HID), f32),
            pltpu.VMEM((2 * HID, 32), f32),
            pltpu.VMEM((16, 2 * HID), f32),
        ],
        compiler_params=pltpu.CompilerParams(
            vmem_limit_bytes=34 * 2**20
        ),
    )(slices, *prepared)

    def total(parts):
        return pl.pallas_call(
            sum_kernel,
            out_shape=shape(parts.shape),
            in_specs=[VMEM],
            out_specs=VMEM,
            compiler_params=room(2),
        )(parts)

    parts = total(exchange(grads, NEAR))
    parts = total(exchange(parts, FAR))
    packed = exchange(parts, NEAR)
    grad_in, grad_mid, grad_out_t = pl.pallas_call(
        unpack_kernel,
        out_shape=(shape((CH + COND, HID)), shape((HID, HID)), shape((4, HID))),
        in_specs=[VMEM],
        out_specs=(pl.BlockSpec(memory_space=pl.ANY),) * 3,
        scratch_shapes=[
            pltpu.VMEM((CH + COND, HID), f32),
            pltpu.VMEM((HID, HID), f32),
            pltpu.VMEM((4, HID), f32),
            pltpu.SemaphoreType.DMA((3,)),
        ],
        compiler_params=room(2),
    )(packed)
    return image[None], grad_in, grad_mid, grad_out_t.T


def solution(mesh):
    torus = Mesh(
        mesh.devices.reshape(2, 2, 8, 4, 2), ("y_far", "y_near", "z", "x", "core")
    )
    return jax.shard_map(
        per_device,
        mesh=torus,
        in_specs=(
            P(BRICK, None, None, None),
            P(VIEW, None),
            P(VIEW, None),
            P(VIEW),
            P(VIEW, None),
            P(),
            P(),
            P(),
            P(VIEW, None, BRICK, None),
        ),
        out_specs=(P(VIEW, None, BRICK, None), P(), P(), P()),
        check_vma=False,
    )
```
